512 devices in a mesh: row: 16 (over y, core), col: 8 (over z), fib: 4 (over x).
Axes of the slice: x: 4, y: 8, z: 8, core: 2. Of those that a mesh axis runs over, the one named last changes fastest.
Arguments:
- values: bfloat16 [768, 12, 128, 128], P(('row', 'col'), 'fib'), may hold values from -3 to 3
- columns: int32 [768, 12], P(('row', 'col')), may hold values from 0 to 767, as said below
- counts: int32 [768], P(('row', 'col')), may hold values from 6 to 12, as said below
Outputs:
- square: bfloat16 [768, 12, 128, 128], P(('row', 'col'), 'fib')
- traces: float32 [2], replicated
The draws below stay inside these ranges and needn't reach their ends.
Inputs may be any that keep to these rules, and one draw needn't show every extreme that they name: Slot 0 of block row i holds i. Every slot s >= 1 of row i, used or not, holds (i + o) mod 768 with 1 <= |o| <= 6, and the columns of one row are distinct. Row i uses slots 0 to counts[i] - 1; later slots are ignored. Some row uses all 12 slots.
All inputs are finite; a program needn't handle non-finite values.
Results may differ from the reference program's by a relative error of at most 0.001.
Values may be sent and summed in bfloat16 or wider, within the bound.
A program may use at most 128 MiB of HBM per device.

```python
import jax
import jax.numpy as jnp
from jax import lax

SLOTS = 12
BLOCK = 128
BAND = 6
NB = 768


def pattern_draw(key):
    base_key = jax.random.fold_in(key, 7)
    key_order, key_count, key_full, key_least = jax.random.split(base_key, 4)
    spread = 2 * BAND
    scores = jax.random.randint(key_order, (NB, spread), 0, 2 ** 20) * spread + jnp.arange(spread, dtype=jnp.int32)[None, :]
    ranked = jnp.argsort(scores, axis=1)[:, :SLOTS - 1].astype(jnp.int32)
    offsets = jnp.where(ranked < BAND, ranked - BAND, ranked - BAND + 1)
    row_ids = jnp.arange(NB, dtype=jnp.int32)[:, None]
    columns = jnp.concatenate([row_ids, (row_ids + offsets) % NB], axis=1).astype(jnp.int32)
    counts = jax.random.randint(key_count, (NB,), SLOTS // 2, SLOTS + 1).astype(jnp.int32)
    full_row = jax.random.randint(key_full, (), 0, NB)
    least_row = (full_row + 1 + jax.random.randint(key_least, (), 0, NB - 1)) % NB
    counts = counts.at[full_row].set(SLOTS).at[least_row].set(SLOTS // 2)
    return (columns, counts)


def draw_columns(key, part):
    return pattern_draw(key)[0]


def draw_counts(key, part):
    return pattern_draw(key)[1]


def draw_values(key, part):
    key_base = jax.random.fold_in(jax.random.fold_in(key, 3), 0)
    shape = (NB, SLOTS, BLOCK, BLOCK)
    entries = jax.random.normal(key_base, shape, jnp.float32) * 0.15
    rising = 0.5 + jnp.arange(NB, dtype=jnp.float32) / NB
    identity = jnp.eye(BLOCK, dtype=jnp.float32)
    entries = entries.at[:, 0].add(rising[:, None, None] * identity[None, :, :])
    return entries.astype(jnp.bfloat16)


def setup_inputs(seed: int = 0) -> dict:
    key_list = jax.random.split(jax.random.key(seed), 4)
    values = draw_values(jax.random.fold_in(key_list[3], 71), 0)
    columns = draw_columns(jax.random.fold_in(key_list[3], 71), 0)
    counts = draw_counts(jax.random.fold_in(key_list[3], 71), 0)
    return dict(values=values, columns=columns, counts=counts)


def reference(values, columns, counts):
    slot_count = columns.shape[1]
    slot_ids = jnp.arange(slot_count, dtype=jnp.int32)

    def one_row(row_id):
        row_cols = columns[row_id]
        keep_mask = slot_ids < counts[row_id]
        picked = values[row_cols].astype(jnp.float32)
        picked_cols = columns[row_cols]
        picked_live = slot_ids[None, :] < counts[row_cols][:, None]
        matches = (picked_cols[:, None, :] == row_cols[None, :, None]) & picked_live[:, None, :]
        matches = matches & keep_mask[:, None, None] & keep_mask[None, :, None]
        chosen = jnp.einsum("ajs,asxy->ajxy", matches.astype(jnp.float32), picked)
        left_tiles = values[row_id].astype(jnp.float32)
        product = jnp.einsum("axy,ajyz->jxz", left_tiles, chosen)
        trace_values = jnp.trace(left_tiles[0])
        trace_square = jnp.trace(product[0])
        return product.astype(jnp.bfloat16), trace_values, trace_square

    square, trace_values, trace_square = lax.map(one_row, jnp.arange(NB, dtype=jnp.int32))
    traces = jnp.stack([jnp.sum(trace_values), jnp.sum(trace_square)])
    return square, traces
```

```python
import functools

import jax
import jax.numpy as jnp
from jax import lax
from jax.experimental import pallas as pl
from jax.experimental.pallas import tpu as pltpu
from jax.sharding import PartitionSpec as P

MESH = pl.DeviceIdType.MESH
BAND = 6
R = 6
T = 3
S = 12
NO = 2 * BAND + 1
B = 128
QB = 32


def kernel(sizes, v_ref, col_ref, cnt_ref, out_ref, tr_ref, L, Q, acc, send, land, tab, ntab, tx, tz, ty,
           stab, sprev, snext, own_s, own_r, rel_s, rel_r, z_s, z_r, tab_s, tab_r, loc, out_s, out_r,
           tx_s, tx_r, tz_s, tz_r, ty_s, ty_r, *halo):
    n_row, n_col, n_fib = sizes
    n_blocks = n_row * n_col * R
    row, col, fib = (lax.axis_index(a) for a in ("row", "col", "fib"))
    group = row * n_col + col

    def along_fib(d):
        return (row, col, lax.rem(fib + d + n_fib, n_fib))

    def along_col(d):
        return (row, lax.rem(col + d, n_col), fib)

    def along_row(d):
        return (lax.rem(row + d, n_row), col, fib)

    def along_group(d):
        other = lax.rem(group + d + n_row * n_col, n_row * n_col)
        return (other // n_col, lax.rem(other, n_col), fib)

    peers = [along_fib(d) for d in range(1, n_fib)] + [along_group(1), along_group(-1)]
    peers += [along_col(d) for d in range(1, n_col)] + [along_row(d) for d in range(1, n_row)]
    barrier = pltpu.get_barrier_semaphore()
    for peer in peers:
        pl.semaphore_signal(barrier, inc=1, device_id=peer, device_id_type=MESH)

    def remote(src, dst, ssem, rsem, device):
        return pltpu.make_async_remote_copy(
            src_ref=src, dst_ref=dst, send_sem=ssem, recv_sem=rsem, device_id=device, device_id_type=MESH
        )

    mine = pl.multiple_of(fib * QB, QB)
    quarter = pl.ds(mine, QB)
    prev, nxt = halo[:R], halo[R:]

    def flip(r, _):
        for t in range(T):
            L[r, T * fib + t] = v_ref[r, t].T
        L[r, S] = jnp.zeros((B, B), jnp.bfloat16)
        return 0

    lax.fori_loop(0, R, flip, 0)
    for ref in halo:
        ref[S] = jnp.zeros((QB, B), jnp.bfloat16)

    rows = lax.broadcasted_iota(jnp.int32, (8, B), 0)
    lanes = lax.broadcasted_iota(jnp.int32, (8, B), 1)
    table, place = jnp.full((8, B), S, jnp.int32), jnp.full((8, B), NO, jnp.int32)
    columns = jnp.concatenate([col_ref[...], jnp.zeros((8 - R, S), jnp.int32)], axis=0)
    counts = jnp.zeros((8, B), jnp.int32)
    for r in range(R):
        counts = jnp.where(rows == r, cnt_ref[r], counts)
    for s in range(S):
        offset = columns[:, s : s + 1] - (group * R + rows) + BAND
        offset = jnp.where(offset < 0, offset + n_blocks, offset)
        offset = jnp.where(offset >= n_blocks, offset - n_blocks, offset)
        table = jnp.where((offset == lanes) & (s < counts), s, table)
        place = jnp.where((lanes == s) & (s < counts), offset, place)
    tab[0:8, :] = table
    tab[8:16, :] = place

    def clear(w, _):
        Q[w, 0:BAND] = jnp.zeros((BAND, QB, B), jnp.bfloat16)
        Q[w, BAND + NO : 2 * BAND + NO] = jnp.zeros((BAND, QB, B), jnp.bfloat16)
        return 0

    lax.fori_loop(0, 3 * R, clear, 0)
    for r in range(R):
        acc[r, NO] = jnp.zeros((QB, B), jnp.float32)

    local = pltpu.make_async_copy(tab, stab, loc.at[0])
    local.start()
    local.wait()
    pl.semaphore_wait(barrier, len(peers))

    def own(r, way):
        part = L.at[r, pl.ds(T * fib, T)]
        return remote(part, part, own_s.at[way, r], own_r.at[way, r], along_fib(1 - 2 * way))

    def relay(r, way):
        cut = 2 - r % 2
        source = lax.rem(fib + (n_fib - 1 if way == 0 else 1), n_fib)
        part = L.at[r, pl.ds(T * source, cut)] if way == 0 else L.at[r, pl.ds(T * source + cut, T - cut)]
        return remote(part, part, rel_s.at[way, r], rel_r.at[way, r], along_fib(1 - 2 * way))

    def shift(r, way):
        dst = (prev if way == 0 else nxt)[r].at[0:S]
        return remote(L.at[r, 0:S, quarter], dst, z_s.at[way, r], z_r.at[way, r], along_group(1 - 2 * way))

    def tables(way):
        return remote(tab.at[0:8], ntab.at[way], tab_s.at[way], tab_r.at[way], along_group(1 - 2 * way))

    for r in range(2):
        own(r, 0).start()
        own(r, 1).start()
    tables(0).start()
    tables(1).start()
    for r in range(R):
        own(r, 0).wait_recv()
        own(r, 1).wait_recv()
        relay(r, 0).start()
        relay(r, 1).start()
        if r + 2 < R:
            own(r + 2, 0).start()
            own(r + 2, 1).start()
        if r >= 1:
            relay(r - 1, 0).wait_recv()
            relay(r - 1, 1).wait_recv()
            shift(r - 1, 0).start()
            shift(r - 1, 1).start()
    relay(R - 1, 0).wait_recv()
    relay(R - 1, 1).wait_recv()
    shift(R - 1, 0).start()
    shift(R - 1, 1).start()

    tables(0).wait_recv()
    tables(1).wait_recv()
    near = (pltpu.make_async_copy(ntab.at[0], sprev, loc.at[1]), pltpu.make_async_copy(ntab.at[1], snext, loc.at[2]))
    for copy in near:
        copy.start()

    def place_own(r, _):
        for o in range(NO):
            Q[R + r, BAND + o] = L[r, stab[r, o], quarter]
        return 0

    lax.fori_loop(0, R, place_own, 0)

    def term(i, w):
        return Q[w, pl.ds(BAND + R + i - w, NO)].reshape(NO * QB, B), L[i, stab[i, w - i]]

    def products(i, window):
        pairs = [term(i, w) for w in window]
        right = jnp.concatenate([p[0] for p in pairs], axis=1)
        left = jnp.concatenate([p[1] for p in pairs], axis=0)
        return jnp.dot(right, left, preferred_element_type=jnp.float32).reshape(NO, QB, B)

    def own_part(i, _):
        acc[i, 0:NO] = products(i, range(R, 2 * R))
        return 0

    lax.fori_loop(0, R, own_part, 0)
    for copy in near:
        copy.wait()
    for r in range(R):
        shift(r, 0).wait_recv()
        shift(r, 1).wait_recv()
        for o in range(NO):
            Q[r, BAND + o] = prev[r][sprev[r, o]]
            Q[2 * R + r, BAND + o] = nxt[r][snext[r, o]]

    def deliver(i, d):
        dst = land.at[i, :, quarter]
        return remote(send.at[d - 1, i], dst, out_s.at[d - 1, i], out_r.at[d - 1, i], along_fib(d))

    diagonal = lax.broadcasted_iota(jnp.int32, (QB, B), 1) == lax.broadcasted_iota(jnp.int32, (QB, B), 0) + mine
    trace_values = jnp.zeros((QB, B), jnp.float32)
    trace_square = jnp.zeros((QB, B), jnp.float32)
    for i in range(R):
        acc[i, 0:NO] += products(i, [*range(i, R), *range(2 * R, 2 * R + i + 1)])
        trace_values += L[i, 0, quarter].astype(jnp.float32)
        trace_square += acc[i, BAND]
        for d in range(n_fib):
            owner = lax.rem(fib + d, n_fib)
            for t in range(T):
                block = acc[i, stab[8 + i, T * owner + t]].astype(jnp.bfloat16)
                if d == 0:
                    land[i, t, quarter] = block
                else:
                    send[d - 1, i, t] = block
        if i >= 1:
            for d in range(1, n_fib):
                deliver(i - 1, d).start()

    def total(tile):
        return jnp.sum(jnp.where(diagonal, tile, 0.0), axis=0, keepdims=True)

    first = jnp.where(rows == 0, total(trace_values), jnp.where(rows == 1, total(trace_square), 0.0))
    tx[fib] = first
    for d in range(1, n_fib):
        deliver(R - 1, d).start()

    def spread(buf, me, size, ssem, rsem, device):
        return [remote(buf.at[me], buf.at[me], ssem.at[d - 1], rsem.at[d - 1], device(d)) for d in range(1, size)]

    def add(buf, size):
        tile = buf[0]
        for k in range(1, size):
            tile += buf[k]
        return tile

    def finish(i):
        for d in range(1, n_fib):
            deliver(i, d).wait_recv()
        for t in range(T):
            out_ref[i, t] = land[i, t].T

    stage_x = spread(tx, fib, n_fib, tx_s, tx_r, along_fib)
    stage_z = spread(tz, col, n_col, tz_s, tz_r, along_col)
    stage_y = spread(ty, row, n_row, ty_s, ty_r, along_row)
    for copy in stage_x:
        copy.start()
    for copy in stage_x:
        copy.wait_recv()
    tz[col] = add(tx, n_fib)
    for copy in stage_z:
        copy.start()
    for copy in stage_z:
        copy.wait_recv()
    ty[row] = add(tz, n_col)
    for copy in stage_y:
        copy.start()
    for i in range(R):
        finish(i)
    for copy in stage_y:
        copy.wait_recv()
    sums = add(ty, n_row)
    tr_ref[0] = jnp.sum(sums[0:1])
    tr_ref[1] = jnp.sum(sums[1:2])

    for copy in [*stage_x, *stage_y, *stage_z, tables(0), tables(1)]:
        copy.wait_send()
    for r in range(R):
        for way in range(2):
            own(r, way).wait_send()
            relay(r, way).wait_send()
            shift(r, way).wait_send()
        for d in range(1, n_fib):
            deliver(r, d).wait_send()


def solution(mesh):
    sizes = tuple(mesh.shape[a] for a in ("row", "col", "fib"))
    bf16, f32, i32 = jnp.bfloat16, jnp.float32, jnp.int32
    dma = pltpu.SemaphoreType.DMA

    def body(values, columns, counts):
        vmem, smem = pl.BlockSpec(memory_space=pltpu.VMEM), pl.BlockSpec(memory_space=pltpu.SMEM)
        return pl.pallas_call(
            functools.partial(kernel, sizes),
            out_shape=(jax.ShapeDtypeStruct((R, T, B, B), bf16), jax.ShapeDtypeStruct((2,), f32)),
            in_specs=[vmem, vmem, smem],
            out_specs=(vmem, smem),
            scratch_shapes=[
                pltpu.VMEM((R, S + 1, B, B), bf16),
                pltpu.VMEM((3 * R, NO + 2 * BAND, QB, B), bf16),
                pltpu.VMEM((R, NO + 1, QB, B), f32),
                pltpu.VMEM((3, R, T, QB, B), bf16),
                pltpu.VMEM((R, T, B, B), bf16),
                pltpu.VMEM((16, B), i32),
                pltpu.VMEM((2, 8, B), i32),
                *(pltpu.VMEM((n, 8, B), f32) for n in (sizes[2], sizes[1], sizes[0])),
                pltpu.SMEM((16, B), i32),
                pltpu.SMEM((8, B), i32),
                pltpu.SMEM((8, B), i32),
                *[dma((2, R))] * 6,
                dma((2,)),
                dma((2,)),
                dma((3,)),
                dma((3, R)),
                dma((3, R)),
                *(dma((n - 1,)) for n in (sizes[2], sizes[2], sizes[1], sizes[1], sizes[0], sizes[0])),
                *[pltpu.VMEM((S + 1, QB, B), bf16)] * (2 * R),
            ],
            compiler_params=pltpu.CompilerParams(collective_id=0, has_side_effects=True),
        )(values, columns, counts)

    in_specs = (P(("row", "col"), "fib", None, None), P(("row", "col"), None), P(("row", "col")))
    out_specs = (P(("row", "col"), "fib", None, None), P())
    return jax.shard_map(body, mesh=mesh, in_specs=in_specs, out_specs=out_specs, check_vma=False)
```

```python
import functools

import jax
import jax.numpy as jnp
from jax import lax
from jax.experimental import pallas as pl
from jax.experimental.pallas import tpu as pltpu
from jax.sharding import PartitionSpec as P

MESH = pl.DeviceIdType.MESH
BAND = 6
R = 6
T = 3
S = 12
NO = 2 * BAND + 1
B = 128
QB = 32


def kernel(sizes, v_ref, col_ref, cnt_ref, out_ref, tr_ref, held, held_s, L, Q, acc, send, land, tab, ntab, tx, tz, ty,
           stab, sprev, snext, own_s, own_r, rel_s, rel_r, z_s, z_r, tab_s, tab_r, loc, out_s, out_r,
           tx_s, tx_r, tz_s, tz_r, ty_s, ty_r, *halo):
    n_row, n_col, n_fib = sizes
    n_blocks = n_row * n_col * R
    row, col, fib = (lax.axis_index(a) for a in ("row", "col", "fib"))
    group = row * n_col + col

    def along_fib(d):
        return (row, col, lax.rem(fib + d + n_fib, n_fib))

    def along_col(d):
        return (row, lax.rem(col + d, n_col), fib)

    def along_row(d):
        return (lax.rem(row + d, n_row), col, fib)

    def along_group(d):
        other = lax.rem(group + d + n_row * n_col, n_row * n_col)
        return (other // n_col, lax.rem(other, n_col), fib)

    peers = [along_fib(d) for d in range(1, n_fib)] + [along_group(1), along_group(-1)]
    peers += [along_col(d) for d in range(1, n_col)] + [along_row(d) for d in range(1, n_row)]
    barrier = pltpu.get_barrier_semaphore()
    for peer in peers:
        pl.semaphore_signal(barrier, inc=1, device_id=peer, device_id_type=MESH)

    def remote(src, dst, ssem, rsem, device):
        return pltpu.make_async_remote_copy(
            src_ref=src, dst_ref=dst, send_sem=ssem, recv_sem=rsem, device_id=device, device_id_type=MESH
        )

    mine = pl.multiple_of(fib * QB, QB)
    quarter = pl.ds(mine, QB)
    prev, nxt = halo[:R], halo[R:]

    fetches = [pltpu.make_async_copy(v_ref.at[r], held.at[r], held_s.at[r]) for r in range(R)]
    for fetch in fetches:
        fetch.start()

    def flip(r):
        fetches[r].wait()
        for t in range(T):
            L[r, T * fib + t] = held[r, t].T

    def own(r, way):
        part = L.at[r, pl.ds(T * fib, T)]
        return remote(part, part, own_s.at[way, r], own_r.at[way, r], along_fib(1 - 2 * way))

    def relay(r, way):
        cut = 2 - r % 2
        source = lax.rem(fib + (n_fib - 1 if way == 0 else 1), n_fib)
        part = L.at[r, pl.ds(T * source, cut)] if way == 0 else L.at[r, pl.ds(T * source + cut, T - cut)]
        return remote(part, part, rel_s.at[way, r], rel_r.at[way, r], along_fib(1 - 2 * way))

    def shift(r, way, d):
        part = pl.ds(T * lax.rem(fib + d, n_fib), T)
        dst = (prev if way == 0 else nxt)[r].at[part]
        return remote(L.at[r, part, quarter], dst, z_s.at[way, r, d], z_r.at[way, r, d], along_group(1 - 2 * way))

    def both(make, *where):
        make(*where[:1], 0, *where[1:]).start()
        make(*where[:1], 1, *where[1:]).start()

    def tables(way):
        return remote(tab.at[0:8], ntab.at[way], tab_s.at[way], tab_r.at[way], along_group(1 - 2 * way))

    flip(0)
    flip(1)
    pl.semaphore_wait(barrier, len(peers))
    both(own, 0)
    both(own, 1)
    for r in range(2, R):
        flip(r)

    rows = lax.broadcasted_iota(jnp.int32, (8, B), 0)
    lanes = lax.broadcasted_iota(jnp.int32, (8, B), 1)
    table, place = jnp.full((8, B), S, jnp.int32), jnp.full((8, B), NO, jnp.int32)
    columns = jnp.concatenate([col_ref[...], jnp.zeros((8 - R, S), jnp.int32)], axis=0)
    counts = jnp.zeros((8, B), jnp.int32)
    for r in range(R):
        counts = jnp.where(rows == r, cnt_ref[r], counts)
    for s in range(S):
        offset = columns[:, s : s + 1] - (group * R + rows) + BAND
        offset = jnp.where(offset < 0, offset + n_blocks, offset)
        offset = jnp.where(offset >= n_blocks, offset - n_blocks, offset)
        table = jnp.where((offset == lanes) & (s < counts), s, table)
        place = jnp.where((lanes == s) & (s < counts), offset, place)
    tab[0:8, :] = table
    tab[8:16, :] = place

    def clear(w, _):
        Q[w, 0:BAND] = jnp.zeros((BAND, QB, B), jnp.bfloat16)
        Q[w, BAND + NO : 2 * BAND + NO] = jnp.zeros((BAND, QB, B), jnp.bfloat16)
        return 0

    lax.fori_loop(0, 3 * R, clear, 0)
    for ref in halo:
        ref[S] = jnp.zeros((QB, B), jnp.bfloat16)
    for r in range(R):
        acc[r, NO] = jnp.zeros((QB, B), jnp.float32)
        L[r, S] = jnp.zeros((B, B), jnp.bfloat16)

    local = pltpu.make_async_copy(tab, stab, loc.at[0])
    local.start()
    for r in range(R):
        both(shift, r, 0)
    tables(0).start()
    tables(1).start()
    for r in range(R):
        own(r, 0).wait_recv()
        own(r, 1).wait_recv()
        both(relay, r)
        if r + 2 < R:
            both(own, r + 2)
        both(shift, r, 1)
        both(shift, r, n_fib - 1)
        if r >= 1:
            relay(r - 1, 0).wait_recv()
            relay(r - 1, 1).wait_recv()
            both(shift, r - 1, 2)
    relay(R - 1, 0).wait_recv()
    relay(R - 1, 1).wait_recv()
    both(shift, R - 1, 2)

    local.wait()
    tables(0).wait_recv()
    tables(1).wait_recv()
    near = (pltpu.make_async_copy(ntab.at[0], sprev, loc.at[1]), pltpu.make_async_copy(ntab.at[1], snext, loc.at[2]))
    for copy in near:
        copy.start()

    def place_own(r, _):
        for o in range(NO):
            Q[R + r, BAND + o] = L[r, stab[r, o], quarter]
        return 0

    lax.fori_loop(0, R, place_own, 0)

    def term(i, w):
        return Q[w, pl.ds(BAND + R + i - w, NO)].reshape(NO * QB, B), L[i, stab[i, w - i]]

    def products(i, window):
        pairs = [term(i, w) for w in window]
        right = jnp.concatenate([p[0] for p in pairs], axis=1)
        left = jnp.concatenate([p[1] for p in pairs], axis=0)
        return jnp.dot(right, left, preferred_element_type=jnp.float32).reshape(NO, QB, B)

    def own_part(i, _):
        acc[i, 0:NO] = products(i, range(R, 2 * R))
        return 0

    lax.fori_loop(0, R, own_part, 0)
    for copy in near:
        copy.wait()
    def take(r):
        for way in range(2):
            for d in range(n_fib):
                shift(r, way, d).wait_recv()
        for o in range(NO):
            Q[r, BAND + o] = prev[r][sprev[r, o]]
            Q[2 * R + r, BAND + o] = nxt[r][snext[r, o]]

    for r in range(R - 1):
        take(r)
    for i in range(R):
        acc[i, 0:NO] += products(i, [*range(i, R - 1), *range(2 * R, 2 * R + min(i, R - 2) + 1)])
    take(R - 1)
    for i in range(R):
        acc[i, 0:NO] += products(i, [R - 1] if i < R - 1 else [R - 1, 3 * R - 1])

    def deliver(i, d):
        dst = land.at[i, :, quarter]
        return remote(send.at[d - 1, i], dst, out_s.at[d - 1, i], out_r.at[d - 1, i], along_fib(d))

    diagonal = lax.broadcasted_iota(jnp.int32, (QB, B), 1) == lax.broadcasted_iota(jnp.int32, (QB, B), 0) + mine
    trace_values = jnp.zeros((QB, B), jnp.float32)
    trace_square = jnp.zeros((QB, B), jnp.float32)
    for i in range(R):
        trace_values += L[i, 0, quarter].astype(jnp.float32)
        trace_square += acc[i, BAND]

    def total(tile):
        return jnp.sum(jnp.where(diagonal, tile, 0.0), axis=0, keepdims=True)

    tx[fib] = jnp.where(rows == 0, total(trace_values), jnp.where(rows == 1, total(trace_square), 0.0))

    def spread(buf, me, size, ssem, rsem, device):
        return [remote(buf.at[me], buf.at[me], ssem.at[d - 1], rsem.at[d - 1], device(d)) for d in range(1, size)]

    def add(buf, size):
        tile = buf[0]
        for k in range(1, size):
            tile += buf[k]
        return tile

    def finish(i):
        for d in range(1, n_fib):
            deliver(i, d).wait_recv()
        for t in range(T):
            out_ref[i, t] = land[i, t].T

    stage_x = spread(tx, fib, n_fib, tx_s, tx_r, along_fib)
    stage_z = spread(tz, col, n_col, tz_s, tz_r, along_col)
    stage_y = spread(ty, row, n_row, ty_s, ty_r, along_row)
    for i in range(R):
        for d in range(n_fib):
            owner = lax.rem(fib + d, n_fib)
            for t in range(T):
                block = acc[i, stab[8 + i, T * owner + t]].astype(jnp.bfloat16)
                if d == 0:
                    land[i, t, quarter] = block
                else:
                    send[d - 1, i, t] = block
        if i == 0:
            for copy in stage_x:
                copy.start()
        else:
            for d in range(1, n_fib):
                deliver(i - 1, d).start()
    for d in range(1, n_fib):
        deliver(R - 1, d).start()
    for copy in stage_x:
        copy.wait_recv()
    tz[col] = add(tx, n_fib)
    for copy in stage_z:
        copy.start()
    for i in range(2):
        finish(i)
    for copy in stage_z:
        copy.wait_recv()
    ty[row] = add(tz, n_col)
    for copy in stage_y:
        copy.start()
    for i in range(2, R):
        finish(i)
    for copy in stage_y:
        copy.wait_recv()
    sums = add(ty, n_row)
    tr_ref[0] = jnp.sum(sums[0:1])
    tr_ref[1] = jnp.sum(sums[1:2])

    for copy in [*stage_x, *stage_y, *stage_z, tables(0), tables(1)]:
        copy.wait_send()
    for r in range(R):
        for way in range(2):
            own(r, way).wait_send()
            relay(r, way).wait_send()
            for d in range(n_fib):
                shift(r, way, d).wait_send()
        for d in range(1, n_fib):
            deliver(r, d).wait_send()


def solution(mesh):
    sizes = tuple(mesh.shape[a] for a in ("row", "col", "fib"))
    bf16, f32, i32 = jnp.bfloat16, jnp.float32, jnp.int32
    dma = pltpu.SemaphoreType.DMA

    def body(values, columns, counts):
        vmem, smem = pl.BlockSpec(memory_space=pltpu.VMEM), pl.BlockSpec(memory_space=pltpu.SMEM)
        return pl.pallas_call(
            functools.partial(kernel, sizes),
            out_shape=(jax.ShapeDtypeStruct((R, T, B, B), bf16), jax.ShapeDtypeStruct((2,), f32)),
            in_specs=[pl.BlockSpec(memory_space=pl.ANY), vmem, smem],
            out_specs=(vmem, smem),
            scratch_shapes=[
                pltpu.VMEM((R, T, B, B), bf16),
                dma((R,)),
                pltpu.VMEM((R, S + 1, B, B), bf16),
                pltpu.VMEM((3 * R, NO + 2 * BAND, QB, B), bf16),
                pltpu.VMEM((R, NO + 1, QB, B), f32),
                pltpu.VMEM((3, R, T, QB, B), bf16),
                pltpu.VMEM((R, T, B, B), bf16),
                pltpu.VMEM((16, B), i32),
                pltpu.VMEM((2, 8, B), i32),
                *(pltpu.VMEM((n, 8, B), f32) for n in (sizes[2], sizes[1], sizes[0])),
                pltpu.SMEM((16, B), i32),
                pltpu.SMEM((8, B), i32),
                pltpu.SMEM((8, B), i32),
                *[dma((2, R))] * 4,
                dma((2, R, sizes[2])),
                dma((2, R, sizes[2])),
                dma((2,)),
                dma((2,)),
                dma((3,)),
                dma((3, R)),
                dma((3, R)),
                *(dma((n - 1,)) for n in (sizes[2], sizes[2], sizes[1], sizes[1], sizes[0], sizes[0])),
                *[pltpu.VMEM((S + 1, QB, B), bf16)] * (2 * R),
            ],
            compiler_params=pltpu.CompilerParams(collective_id=0, has_side_effects=True),
        )(values, columns, counts)

    in_specs = (P(("row", "col"), "fib", None, None), P(("row", "col"), None), P(("row", "col")))
    out_specs = (P(("row", "col"), "fib", None, None), P())
    return jax.shard_map(body, mesh=mesh, in_specs=in_specs, out_specs=out_specs, check_vma=False)
```

```python
import functools

import jax
import jax.numpy as jnp
from jax import lax
from jax.experimental import pallas as pl
from jax.experimental.pallas import tpu as pltpu
from jax.sharding import PartitionSpec as P

MESH = pl.DeviceIdType.MESH
BAND = 6
R = 6
T = 3
S = 12
NO = 2 * BAND + 1
B = 128
QB = 32


def kernel(sizes, v_ref, col_ref, cnt_ref, land, ty, held, col_v, cnt_v, L, Q, acc, send, tab, ntab, tx, tz,
           stab, sprev, snext, held_s, loc, own_r, rel_r, z_r, out_r, once, *halo):
    n_row, n_col, n_fib = sizes
    n_blocks = n_row * n_col * R
    row, col, fib = (lax.axis_index(a) for a in ("row", "col", "fib"))
    group = row * n_col + col

    def along_fib(d):
        return (row, col, lax.rem(fib + d + n_fib, n_fib))

    def along_col(d):
        return (row, lax.rem(col + d, n_col), fib)

    def along_row(d):
        return (lax.rem(row + d, n_row), col, fib)

    def along_group(d):
        other = lax.rem(group + d + n_row * n_col, n_row * n_col)
        return (other // n_col, lax.rem(other, n_col), fib)

    peers = [along_fib(d) for d in range(1, n_fib)] + [along_group(1), along_group(-1)]
    peers += [along_col(d) for d in range(1, n_col)] + [along_row(d) for d in range(1, n_row)]
    barrier = pltpu.get_barrier_semaphore()
    for peer in peers:
        pl.semaphore_signal(barrier, inc=1, device_id=peer, device_id_type=MESH)

    def remote(src, dst, ssem, rsem, device):
        return pltpu.make_async_remote_copy(
            src_ref=src, dst_ref=dst, send_sem=ssem, recv_sem=rsem, device_id=device, device_id_type=MESH
        )

    mine = pl.multiple_of(fib * QB, QB)
    quarter = pl.ds(mine, QB)
    prev, nxt = halo[:R], halo[R:]

    (own_s, rel_s, z_s, tab_s, tab_r, out_s, tx_s, tx_r, tz_s, tz_r, ty_s, ty_r) = (once.at[k] for k in range(12))
    whole = [
        pltpu.make_async_copy(col_ref, col_v, loc.at[0]),
        pltpu.make_async_copy(cnt_ref, cnt_v, loc.at[1]),
    ]
    fetches = [pltpu.make_async_copy(v_ref.at[r], held.at[r], held_s.at[r]) for r in range(R)]
    for fetch in fetches + whole:
        fetch.start()

    def flip(r):
        fetches[r].wait()
        for t in range(T):
            L[r, T * fib + t] = held[r, t].T

    def own(r, way):
        part = L.at[r, pl.ds(T * fib, T)]
        return remote(part, part, own_s, own_r.at[r], along_fib(1 - 2 * way))

    def relay(r, way):
        cut = 2 - r % 2
        source = lax.rem(fib + (n_fib - 1 if way == 0 else 1), n_fib)
        part = L.at[r, pl.ds(T * source, cut)] if way == 0 else L.at[r, pl.ds(T * source + cut, T - cut)]
        return remote(part, part, rel_s, rel_r.at[r], along_fib(1 - 2 * way))

    def shift(r, way, d):
        part = pl.ds(T * lax.rem(fib + d, n_fib), T)
        dst = (prev if way == 0 else nxt)[r].at[part]
        return remote(L.at[r, part, quarter], dst, z_s, z_r.at[r // (R - 1)], along_group(1 - 2 * way))

    def drain(ref, sem):
        pltpu.make_async_copy(ref, ref, sem).wait()

    def both(make, *where):
        make(*where[:1], 0, *where[1:]).start()
        make(*where[:1], 1, *where[1:]).start()

    def tables(way):
        return remote(tab.at[0:8], ntab.at[way], tab_s, tab_r, along_group(1 - 2 * way))

    flip(0)
    flip(1)
    pl.semaphore_wait(barrier, len(peers))
    both(own, 0)
    both(own, 1)
    for r in range(2, R):
        flip(r)

    for copy in whole:
        copy.wait()
    rows = lax.broadcasted_iota(jnp.int32, (8, B), 0)
    lanes = lax.broadcasted_iota(jnp.int32, (8, B), 1)
    table, place = jnp.full((8, B), S, jnp.int32), jnp.full((8, B), NO, jnp.int32)
    columns = jnp.concatenate([col_v[...], jnp.zeros((8 - R, S), jnp.int32)], axis=0)
    counts = jnp.zeros((8, B), jnp.int32)
    for r in range(R):
        counts = jnp.where(rows == r, cnt_v[r], counts)
    for s in range(S):
        offset = columns[:, s : s + 1] - (group * R + rows) + BAND
        offset = jnp.where(offset < 0, offset + n_blocks, offset)
        offset = jnp.where(offset >= n_blocks, offset - n_blocks, offset)
        table = jnp.where((offset == lanes) & (s < counts), s, table)
        place = jnp.where((lanes == s) & (s < counts), offset, place)
    tab[0:8, :] = table
    tab[8:16, :] = place

    def clear(w, _):
        Q[w, 0:BAND] = jnp.zeros((BAND, QB, B), jnp.bfloat16)
        Q[w, BAND + NO : 2 * BAND + NO] = jnp.zeros((BAND, QB, B), jnp.bfloat16)
        return 0

    lax.fori_loop(0, 3 * R, clear, 0)
    for ref in halo:
        ref[S] = jnp.zeros((QB, B), jnp.bfloat16)
    for r in range(R):
        acc[r, NO] = jnp.zeros((QB, B), jnp.float32)
        L[r, S] = jnp.zeros((B, B), jnp.bfloat16)

    local = pltpu.make_async_copy(tab, stab, loc.at[2])
    local.start()
    for r in range(R):
        both(shift, r, 0)
    tables(0).start()
    tables(1).start()
    for r in range(R):
        drain(L.at[r, 0 : 2 * T], own_r.at[r])
        both(relay, r)
        if r + 2 < R:
            both(own, r + 2)
        both(shift, r, 1)
        both(shift, r, n_fib - 1)
        if r >= 1:
            drain(L.at[r, 0:T], rel_r.at[r - 1])
            both(shift, r - 1, 2)
    drain(L.at[0, 0:T], rel_r.at[R - 1])
    both(shift, R - 1, 2)

    local.wait()
    drain(ntab, tab_r)
    near = (pltpu.make_async_copy(ntab.at[0], sprev, loc.at[0]), pltpu.make_async_copy(ntab.at[1], snext, loc.at[1]))
    for copy in near:
        copy.start()

    def place_own(r, _):
        for o in range(NO):
            Q[R + r, BAND + o] = L[r, stab[r, o], quarter]
        return 0

    lax.fori_loop(0, R, place_own, 0)

    def term(i, w):
        return Q[w, pl.ds(BAND + R + i - w, NO)].reshape(NO * QB, B), L[i, stab[i, w - i]]

    def products(i, window):
        pairs = [term(i, w) for w in window]
        right = jnp.concatenate([p[0] for p in pairs], axis=1)
        left = jnp.concatenate([p[1] for p in pairs], axis=0)
        return jnp.dot(right, left, preferred_element_type=jnp.float32).reshape(NO, QB, B)

    def own_part(i, _):
        acc[i, 0:NO] = products(i, range(R, 2 * R))
        return 0

    lax.fori_loop(0, R, own_part, 0)
    for copy in near:
        copy.wait()
    def take(r):
        for o in range(NO):
            Q[r, BAND + o] = prev[r][sprev[r, o]]
            Q[2 * R + r, BAND + o] = nxt[r][snext[r, o]]

    drain(L.at[0 : R - 1, 0 : S // 2], z_r.at[0])
    for r in range(R - 1):
        take(r)
    for i in range(R):
        acc[i, 0:NO] += products(i, [*range(i, R - 1), *range(2 * R, 2 * R + min(i, R - 2) + 1)])
    drain(L.at[0, 0 : S // 2], z_r.at[1])
    take(R - 1)
    for i in range(R):
        acc[i, 0:NO] += products(i, [R - 1] if i < R - 1 else [R - 1, 3 * R - 1])

    def deliver(i, d):
        dst = land.at[i, :, quarter]
        return remote(send.at[d - 1, i], dst, out_s, out_r.at[i], along_fib(d))

    diagonal = lax.broadcasted_iota(jnp.int32, (QB, B), 1) == lax.broadcasted_iota(jnp.int32, (QB, B), 0) + mine
    trace_values = jnp.zeros((QB, B), jnp.float32)
    trace_square = jnp.zeros((QB, B), jnp.float32)
    for i in range(R):
        trace_values += L[i, 0, quarter].astype(jnp.float32)
        trace_square += acc[i, BAND]

    def total(tile):
        return jnp.sum(jnp.where(diagonal, tile, 0.0), axis=0, keepdims=True)

    tx[fib] = jnp.where(rows == 0, total(trace_values), jnp.where(rows == 1, total(trace_square), 0.0))

    def spread(buf, me, size, ssem, rsem, device):
        return [remote(buf.at[me], buf.at[me], ssem, rsem, device(d)) for d in range(1, size)]

    def add(buf, size):
        tile = buf[0]
        for k in range(1, size):
            tile += buf[k]
        return tile

    stage_x = spread(tx, fib, n_fib, tx_s, tx_r, along_fib)
    stage_z = spread(tz, col, n_col, tz_s, tz_r, along_col)
    stage_y = spread(ty, row, n_row, ty_s, ty_r, along_row)
    for i in range(R):
        for d in range(n_fib):
            owner = lax.rem(fib + d, n_fib)
            for t in range(T):
                block = acc[i, stab[8 + i, T * owner + t]].astype(jnp.bfloat16)
                if d == 0:
                    land[i, t, quarter] = block
                else:
                    send[d - 1, i, t] = block
        if i == 0:
            for copy in stage_x:
                copy.start()
        else:
            for d in range(1, n_fib):
                deliver(i - 1, d).start()
    for d in range(1, n_fib):
        deliver(R - 1, d).start()
    drain(tx.at[1:n_fib], tx_r)
    tz[col] = add(tx, n_fib)
    for copy in stage_z:
        copy.start()
    drain(tz.at[1:n_col], tz_r)
    ty[row] = add(tz, n_col)
    for copy in stage_y:
        copy.start()

    drain(L.at[0:R, 0 : 2 * T], own_s)
    drain(L.at[0:R, 0:T], rel_s)
    drain(L.at[0:R, 0 : S // 2], z_s)
    drain(tab, tab_s)
    drain(send, out_s)
    drain(tx.at[1:n_fib], tx_s)
    drain(tz.at[1:n_col], tz_s)
    for i in range(R):
        drain(land.at[i, :, 0 : B - QB], out_r.at[i])
    drain(ty.at[1:n_row], ty_r)
    drain(ty.at[1:n_row], ty_s)


def finish(land, ty, out_ref, tr_ref, out_v, sem):
    copies = []
    for i in range(R):
        for t in range(T):
            out_v[i, t] = land[i, t].T
        copies.append(pltpu.make_async_copy(out_v.at[i], out_ref.at[i], sem.at[i]))
        if i:
            copies[i - 1].start()
    copies[R - 1].start()
    sums = ty[0]
    for k in range(1, ty.shape[0]):
        sums += ty[k]
    tr_ref[0] = jnp.sum(sums[0:1])
    tr_ref[1] = jnp.sum(sums[1:2])
    for copy in copies:
        copy.wait()


def solution(mesh):
    sizes = tuple(mesh.shape[a] for a in ("row", "col", "fib"))
    bf16, f32, i32 = jnp.bfloat16, jnp.float32, jnp.int32
    dma = pltpu.SemaphoreType.DMA

    def body(values, columns, counts):
        vmem, smem = pl.BlockSpec(memory_space=pltpu.VMEM), pl.BlockSpec(memory_space=pltpu.SMEM)
        hbm = pl.BlockSpec(memory_space=pl.ANY)
        land, ty = pl.pallas_call(
            functools.partial(kernel, sizes),
            out_shape=(pltpu.VMEM((R, T, B, B), bf16), pltpu.VMEM((sizes[0], 8, B), f32)),
            in_specs=[hbm, hbm, hbm],
            out_specs=(vmem, vmem),
            scratch_shapes=[
                pltpu.VMEM((R, T, B, B), bf16),
                pltpu.VMEM((R, S), i32),
                pltpu.SMEM((R,), i32),
                pltpu.VMEM((R, S + 1, B, B), bf16),
                pltpu.VMEM((3 * R, NO + 2 * BAND, QB, B), bf16),
                pltpu.VMEM((R, NO + 1, QB, B), f32),
                pltpu.VMEM((3, R, T, QB, B), bf16),
                pltpu.VMEM((16, B), i32),
                pltpu.VMEM((2, 8, B), i32),
                pltpu.VMEM((sizes[2], 8, B), f32),
                pltpu.VMEM((sizes[1], 8, B), f32),
                pltpu.SMEM((16, B), i32),
                pltpu.SMEM((8, B), i32),
                pltpu.SMEM((8, B), i32),
                dma((R,)),
                dma((3,)),
                dma((R,)),
                dma((R,)),
                dma((2,)),
                dma((R,)),
                dma((12,)),
                *[pltpu.VMEM((S + 1, QB, B), bf16)] * (2 * R),
            ],
            compiler_params=pltpu.CompilerParams(collective_id=0, has_side_effects=True),
        )(values, columns, counts)
        return pl.pallas_call(
            finish,
            out_shape=(jax.ShapeDtypeStruct((R, T, B, B), bf16), jax.ShapeDtypeStruct((2,), f32)),
            in_specs=[vmem, vmem],
            out_specs=(hbm, smem),
            scratch_shapes=[pltpu.VMEM((R, T, B, B), bf16), dma((R,))],
        )(*(pltpu.with_memory_space_constraint(a, pltpu.VMEM) for a in (land, ty)))

    in_specs = (P(("row", "col"), "fib", None, None), P(("row", "col"), None), P(("row", "col")))
    out_specs = (P(("row", "col"), "fib", None, None), P())
    return jax.shard_map(body, mesh=mesh, in_specs=in_specs, out_specs=out_specs, check_vma=False)
```

```python
import functools

import jax
import jax.numpy as jnp
from jax import lax
from jax.experimental import pallas as pl
from jax.experimental.pallas import tpu as pltpu
from jax.sharding import PartitionSpec as P

MESH = pl.DeviceIdType.MESH
BAND = 6
R = 6
T = 3
S = 12
NO = 2 * BAND + 1
B = 128
QB = 32


def kernel(sizes, v_ref, col_ref, cnt_ref, land, ty, held, col_v, cnt_v, E, Q, acc, send, tab, ntab, tx, tz,
           stab, sprev, snext, held_s, loc, own_r, rel_r, z_r, out_r, once, known, *buffers):
    n_row, n_col, n_fib = sizes
    n_blocks = n_row * n_col * R
    row, col, fib = (lax.axis_index(a) for a in ("row", "col", "fib"))
    group = row * n_col + col

    def along_fib(d):
        return (row, col, lax.rem(fib + d + n_fib, n_fib))

    def along_col(d):
        return (row, lax.rem(col + d, n_col), fib)

    def along_row(d):
        return (lax.rem(row + d, n_row), col, fib)

    def along_group(d):
        other = lax.rem(group + d + n_row * n_col, n_row * n_col)
        return (other // n_col, lax.rem(other, n_col), fib)

    beside = [along_col(1), along_col(n_col - 1), *(along_row(d) for d in (1, 2, n_row - 2, n_row - 1))]
    peers = [along_fib(d) for d in range(1, n_fib)] + [along_group(1), along_group(-1)] + beside
    barrier = pltpu.get_barrier_semaphore()
    for peer in peers:
        pl.semaphore_signal(barrier, inc=1, device_id=peer, device_id_type=MESH)

    def remote(src, dst, ssem, rsem, device):
        return pltpu.make_async_remote_copy(
            src_ref=src, dst_ref=dst, send_sem=ssem, recv_sem=rsem, device_id=device, device_id_type=MESH
        )

    mine = pl.multiple_of(fib * QB, QB)
    quarter = pl.ds(mine, QB)
    L, halo = buffers[:R], buffers[R:]
    prev, nxt = halo[:R], halo[R:]

    (own_s, rel_s, z_s, tab_s, tab_r, out_s, tx_s, tx_r, tz_s, tz_r, ty_s, ty_r, e_s, e_r) = (
        once.at[k] for k in range(14)
    )
    whole = [
        pltpu.make_async_copy(col_ref, col_v, loc.at[0]),
        pltpu.make_async_copy(cnt_ref, cnt_v, loc.at[1]),
    ]
    fetches = [pltpu.make_async_copy(v_ref.at[r], held.at[r], held_s.at[r]) for r in range(R)]
    for fetch in fetches + whole:
        fetch.start()

    def flip(r):
        fetches[r].wait()
        for t in range(T):
            L[r][T * fib + t] = held[r, t].T

    def own(r, way):
        part = L[r].at[pl.ds(T * fib, T)]
        return remote(part, part, own_s, own_r.at[r], along_fib(1 - 2 * way))

    def relay(r, way):
        cut = 2 - r % 2
        source = lax.rem(fib + (n_fib - 1 if way == 0 else 1), n_fib)
        part = L[r].at[pl.ds(T * source, cut)] if way == 0 else L[r].at[pl.ds(T * source + cut, T - cut)]
        return remote(part, part, rel_s, rel_r.at[r], along_fib(1 - 2 * way))

    def shift(r, way, d):
        part = pl.ds(T * lax.rem(fib + d, n_fib), T)
        dst = (prev if way == 0 else nxt)[r].at[part]
        src = E.at[part] if r == R - 1 and d else L[r].at[part, quarter]
        return remote(src, dst, z_s, z_r.at[r // (R - 2)], along_group(1 - 2 * way))

    def early(d):
        theirs = pl.ds(pl.multiple_of(lax.rem(fib + d, n_fib) * QB, QB), QB)
        part = pl.ds(T * fib, T)
        return remote(L[R - 1].at[part, theirs], E.at[part], e_s, e_r, along_fib(d))

    def drain(ref, sem):
        pltpu.make_async_copy(ref, ref, sem).wait()

    def both(make, *where):
        make(*where[:1], 0, *where[1:]).start()
        make(*where[:1], 1, *where[1:]).start()

    def tables(way):
        return remote(tab.at[0:8], ntab.at[way], tab_s, tab_r, along_group(1 - 2 * way))

    flip(0)
    flip(1)
    pl.semaphore_wait(barrier, len(peers))
    both(own, 0)
    both(own, 1)
    for r in range(2, R):
        flip(r)
    for d in range(1, n_fib):
        early(d).start()

    for copy in whole:
        copy.wait()
    rows = lax.broadcasted_iota(jnp.int32, (8, B), 0)
    lanes = lax.broadcasted_iota(jnp.int32, (8, B), 1)
    table, place = jnp.full((8, B), S, jnp.int32), jnp.full((8, B), NO, jnp.int32)
    columns = jnp.concatenate([col_v[...], jnp.zeros((8 - R, S), jnp.int32)], axis=0)
    counts = jnp.zeros((8, B), jnp.int32)
    for r in range(R):
        counts = jnp.where(rows == r, cnt_v[r], counts)
    for s in range(S):
        offset = columns[:, s : s + 1] - (group * R + rows) + BAND
        offset = jnp.where(offset < 0, offset + n_blocks, offset)
        offset = jnp.where(offset >= n_blocks, offset - n_blocks, offset)
        table = jnp.where((offset == lanes) & (s < counts), s, table)
        place = jnp.where((lanes == s) & (s < counts), offset, place)
    tab[0:8, :] = table
    tab[8:16, :] = place

    def clear(w, _):
        Q[w, 0:BAND] = jnp.zeros((BAND, QB, B), jnp.bfloat16)
        Q[w, BAND + NO : 2 * BAND + NO] = jnp.zeros((BAND, QB, B), jnp.bfloat16)
        return 0

    lax.fori_loop(0, 3 * R, clear, 0)
    for ref in halo:
        ref[S] = jnp.zeros((QB, B), jnp.bfloat16)
    for r in range(R):
        acc[r, NO] = jnp.zeros((QB, B), jnp.float32)
        L[r][S] = jnp.zeros((B, B), jnp.bfloat16)

    local = pltpu.make_async_copy(tab, stab, loc.at[2])
    local.start()
    for r in range(R):
        both(shift, r, 0)
    tables(0).start()
    tables(1).start()
    near = (pltpu.make_async_copy(ntab.at[0], sprev, loc.at[0]), pltpu.make_async_copy(ntab.at[1], snext, loc.at[1]))

    def term(i, w):
        return Q[w, pl.ds(BAND + R + i - w, NO)].reshape(NO * QB, B), L[i][stab[i, w - i]]

    def products(i, window):
        pairs = [term(i, w) for w in window]
        right = jnp.concatenate([p[0] for p in pairs], axis=1)
        left = jnp.concatenate([p[1] for p in pairs], axis=0)
        return jnp.dot(right, left, preferred_element_type=jnp.float32).reshape(NO, QB, B)

    def within(r):
        for o in range(NO):
            Q[R + r, BAND + o] = L[r][stab[r, o], quarter]
        acc[r, 0:NO] = products(r, range(R, R + r + 1))
        for i in range(r):
            acc[i, 0:NO] += products(i, [R + r])

    def take(r):
        for o in range(NO):
            Q[r, BAND + o] = prev[r][sprev[r, o]]
            Q[2 * R + r, BAND + o] = nxt[r][snext[r, o]]

    def tell(k):
        for peer in beside:
            pl.semaphore_signal(known.at[k], inc=1, device_id=peer, device_id_type=MESH)

    tell(0)
    for r in range(R):
        drain(L[r].at[0 : 2 * T], own_r.at[r])
        both(relay, r)
        if r + 2 < R:
            both(own, r + 2)
        if r < R - 1:
            both(shift, r, 1)
            both(shift, r, n_fib - 1)
        if r == 1:
            drain(E.at[0 : S - T], e_r)
            for d in range(1, n_fib):
                both(shift, R - 1, d)
            local.wait()
        if r >= 1:
            drain(L[r].at[0:T], rel_r.at[r - 1])
            both(shift, r - 1, 2)
            within(r - 1)
        if 2 <= r < 5:
            pl.semaphore_wait(known.at[r - 2], len(beside))
            if r < 4:
                tell(r - 1)
    drain(ntab, tab_r)
    for copy in near:
        copy.start()
    drain(Q.at[0 : 2 * R, 0 : 2 * n_fib], z_r.at[0])
    for copy in near:
        copy.wait()
    for r in range(R - 2):
        take(r)
    for i in range(R - 1):
        acc[i, 0:NO] += products(i, [*range(i, R - 2), *range(2 * R, 2 * R + min(i, R - 3) + 1)])
    drain(L[R - 1].at[0:T], rel_r.at[R - 1])
    within(R - 1)
    drain(Q.at[0:R, 0 : 2 * n_fib], z_r.at[1])
    take(R - 2)
    take(R - 1)
    for i in range(R):
        late = [w for w in (R - 2, R - 1) if w >= i] + [2 * R + w for w in (R - 2, R - 1) if w <= i]
        acc[i, 0:NO] += products(i, late if i < R - 1 else [R - 1, *range(2 * R, 3 * R)])

    def deliver(i, d):
        dst = land.at[i, :, quarter]
        return remote(send.at[d - 1, i], dst, out_s, out_r.at[i], along_fib(d))

    diagonal = lax.broadcasted_iota(jnp.int32, (QB, B), 1) == lax.broadcasted_iota(jnp.int32, (QB, B), 0) + mine
    trace_values = jnp.zeros((QB, B), jnp.float32)
    trace_square = jnp.zeros((QB, B), jnp.float32)
    for i in range(R):
        trace_values += L[i][0, quarter].astype(jnp.float32)
        trace_square += acc[i, BAND]

    def total(tile):
        return jnp.sum(jnp.where(diagonal, tile, 0.0), axis=0, keepdims=True)

    tx[fib] = jnp.where(rows == 0, total(trace_values), jnp.where(rows == 1, total(trace_square), 0.0))

    def spread(buf, me, size, ssem, rsem, device):
        return [remote(buf.at[me], buf.at[me], ssem, rsem, device(d)) for d in range(1, size)]

    def add(buf, size):
        tile = buf[0]
        for k in range(1, size):
            tile += buf[k]
        return tile

    stage_x = spread(tx, fib, n_fib, tx_s, tx_r, along_fib)
    stage_z = spread(tz, col, n_col, tz_s, tz_r, along_col)
    stage_y = spread(ty, row, n_row, ty_s, ty_r, along_row)
    for i in range(R):
        for d in range(n_fib):
            owner = lax.rem(fib + d, n_fib)
            for t in range(T):
                block = acc[i, stab[8 + i, T * owner + t]].astype(jnp.bfloat16)
                if d == 0:
                    land[i, t, quarter] = block
                else:
                    send[d - 1, i, t] = block
        if i == 0:
            for copy in stage_x:
                copy.start()
        else:
            for d in range(1, n_fib):
                deliver(i - 1, d).start()
    for d in range(1, n_fib):
        deliver(R - 1, d).start()
    drain(tx.at[1:n_fib], tx_r)
    tz[col] = add(tx, n_fib)
    for copy in stage_z:
        copy.start()
    drain(tz.at[1:n_col], tz_r)
    ty[row] = add(tz, n_col)
    for copy in stage_y:
        copy.start()

    drain(Q.at[:, 0 : 2 * n_fib], own_s)
    drain(Q.at[:, 0:n_fib], rel_s)
    drain(Q.at[:, 0 : 2 * n_fib], z_s)
    drain(E.at[0 : S - T], e_s)
    drain(tab, tab_s)
    drain(send, out_s)
    drain(tx.at[1:n_fib], tx_s)
    drain(tz.at[1:n_col], tz_s)
    for i in range(R):
        drain(land.at[i, :, 0 : B - QB], out_r.at[i])
    drain(ty.at[1:n_row], ty_r)
    drain(ty.at[1:n_row], ty_s)


def finish(land, ty, out_ref, tr_ref, out_v, sem):
    copies = []
    for i in range(R):
        for t in range(T):
            out_v[i, t] = land[i, t].T
        copies.append(pltpu.make_async_copy(out_v.at[i], out_ref.at[i], sem.at[i]))
        if i:
            copies[i - 1].start()
    copies[R - 1].start()
    sums = ty[0]
    for k in range(1, ty.shape[0]):
        sums += ty[k]
    tr_ref[0] = jnp.sum(sums[0:1])
    tr_ref[1] = jnp.sum(sums[1:2])
    for copy in copies:
        copy.wait()


def solution(mesh):
    sizes = tuple(mesh.shape[a] for a in ("row", "col", "fib"))
    bf16, f32, i32 = jnp.bfloat16, jnp.float32, jnp.int32
    dma = pltpu.SemaphoreType.DMA

    def body(values, columns, counts):
        vmem, smem = pl.BlockSpec(memory_space=pltpu.VMEM), pl.BlockSpec(memory_space=pltpu.SMEM)
        hbm = pl.BlockSpec(memory_space=pl.ANY)
        land, ty = pl.pallas_call(
            functools.partial(kernel, sizes),
            out_shape=(pltpu.VMEM((R, T, B, B), bf16), pltpu.VMEM((sizes[0], 8, B), f32)),
            in_specs=[hbm, hbm, hbm],
            out_specs=(vmem, vmem),
            scratch_shapes=[
                pltpu.VMEM((R, T, B, B), bf16),
                pltpu.VMEM((R, S), i32),
                pltpu.SMEM((R,), i32),
                pltpu.VMEM((S, QB, B), bf16),
                pltpu.VMEM((3 * R, NO + 2 * BAND, QB, B), bf16),
                pltpu.VMEM((R, NO + 1, QB, B), f32),
                pltpu.VMEM((3, R, T, QB, B), bf16),
                pltpu.VMEM((16, B), i32),
                pltpu.VMEM((2, 8, B), i32),
                pltpu.VMEM((sizes[2], 8, B), f32),
                pltpu.VMEM((sizes[1], 8, B), f32),
                pltpu.SMEM((16, B), i32),
                pltpu.SMEM((8, B), i32),
                pltpu.SMEM((8, B), i32),
                dma((R,)),
                dma((3,)),
                dma((R,)),
                dma((R,)),
                dma((2,)),
                dma((R,)),
                dma((14,)),
                pltpu.SemaphoreType.REGULAR((3,)),
                *[pltpu.VMEM((S + 1, B, B), bf16)] * R,
                *[pltpu.VMEM((S + 1, QB, B), bf16)] * (2 * R),
            ],
            compiler_params=pltpu.CompilerParams(collective_id=0, has_side_effects=True),
        )(values, columns, counts)
        return pl.pallas_call(
            finish,
            out_shape=(jax.ShapeDtypeStruct((R, T, B, B), bf16), jax.ShapeDtypeStruct((2,), f32)),
            in_specs=[vmem, vmem],
            out_specs=(hbm, smem),
            scratch_shapes=[pltpu.VMEM((R, T, B, B), bf16), dma((R,))],
        )(*(pltpu.with_memory_space_constraint(a, pltpu.VMEM) for a in (land, ty)))

    in_specs = (P(("row", "col"), "fib", None, None), P(("row", "col"), None), P(("row", "col")))
    out_specs = (P(("row", "col"), "fib", None, None), P())
    return jax.shard_map(body, mesh=mesh, in_specs=in_specs, out_specs=out_specs, check_vma=False)
```

```python
import functools

import jax
import jax.numpy as jnp
from jax import lax
from jax.experimental import pallas as pl
from jax.experimental.pallas import tpu as pltpu
from jax.sharding import PartitionSpec as P

MESH = pl.DeviceIdType.MESH
BAND = 6
R = 6
T = 3
S = 12
NO = 2 * BAND + 1
B = 128
QB = 32


def kernel(sizes, v_ref, col_ref, cnt_ref, land, ty, held, col_v, cnt_v, E, Q, acc, send, tab, ntab, tx, tz,
           stab, sprev, snext, held_s, loc, own_r, rel_r, z_r, out_r, once, known, *buffers):
    n_row, n_col, n_fib = sizes
    n_blocks = n_row * n_col * R
    row, col, fib = (lax.axis_index(a) for a in ("row", "col", "fib"))
    group = row * n_col + col

    def along_fib(d):
        return (row, col, lax.rem(fib + d + n_fib, n_fib))

    def along_col(d):
        return (row, lax.rem(col + d, n_col), fib)

    def along_row(d):
        return (lax.rem(row + d, n_row), col, fib)

    def along_group(d):
        other = lax.rem(group + d + n_row * n_col, n_row * n_col)
        return (other // n_col, lax.rem(other, n_col), fib)

    beside = [along_col(1), along_col(n_col - 1), *(along_row(d) for d in (1, 2, n_row - 2, n_row - 1))]
    core = lax.rem(row, 2)

    def along_line(d):
        return (row - core + lax.rem(core + d, 2), col, lax.rem(fib + d // 2, n_fib))

    peers = [along_line(d) for d in range(1, 2 * n_fib)] + [along_fib(d) for d in range(1, n_fib)] + [along_group(1), along_group(-1)] + beside
    barrier = pltpu.get_barrier_semaphore()
    for peer in peers:
        pl.semaphore_signal(barrier, inc=1, device_id=peer, device_id_type=MESH)

    def remote(src, dst, ssem, rsem, device):
        return pltpu.make_async_remote_copy(
            src_ref=src, dst_ref=dst, send_sem=ssem, recv_sem=rsem, device_id=device, device_id_type=MESH
        )

    mine = pl.multiple_of(fib * QB, QB)
    quarter = pl.ds(mine, QB)
    L, halo = buffers[:R], buffers[R:]
    prev, nxt = halo[:R], halo[R:]

    (own_s, rel_s, z_s, tab_s, tab_r, out_s, tx_s, tx_r, tz_s, tz_r, ty_s, ty_r, e_s, e_r) = (
        once.at[k] for k in range(14)
    )
    whole = [
        pltpu.make_async_copy(col_ref, col_v, loc.at[0]),
        pltpu.make_async_copy(cnt_ref, cnt_v, loc.at[1]),
    ]
    fetches = [pltpu.make_async_copy(v_ref.at[r], held.at[r], held_s.at[r]) for r in range(R)]
    for fetch in fetches + whole:
        fetch.start()

    def flip(r):
        fetches[r].wait()
        for t in range(T):
            L[r][T * fib + t] = held[r, t].T

    def own(r, way):
        part = L[r].at[pl.ds(T * fib, T)]
        return remote(part, part, own_s, own_r.at[r], along_fib(1 - 2 * way))

    def relay(r, way):
        cut = 2 - r % 2
        source = lax.rem(fib + (n_fib - 1 if way == 0 else 1), n_fib)
        part = L[r].at[pl.ds(T * source, cut)] if way == 0 else L[r].at[pl.ds(T * source + cut, T - cut)]
        return remote(part, part, rel_s, rel_r.at[r], along_fib(1 - 2 * way))

    def shift(r, way, d):
        part = pl.ds(T * lax.rem(fib + d, n_fib), T)
        dst = (prev if way == 0 else nxt)[r].at[part]
        src = E.at[part] if r == R - 1 and d else L[r].at[part, quarter]
        return remote(src, dst, z_s, z_r.at[r // (R - 2)], along_group(1 - 2 * way))

    def early(d):
        theirs = pl.ds(pl.multiple_of(lax.rem(fib + d, n_fib) * QB, QB), QB)
        part = pl.ds(T * fib, T)
        return remote(L[R - 1].at[part, theirs], E.at[part], e_s, e_r, along_fib(d))

    def drain(ref, sem):
        pltpu.make_async_copy(ref, ref, sem).wait()

    def both(make, *where):
        make(*where[:1], 0, *where[1:]).start()
        make(*where[:1], 1, *where[1:]).start()

    def tables(way):
        return remote(tab.at[0:8], ntab.at[way], tab_s, tab_r, along_group(1 - 2 * way))

    flip(0)
    flip(1)
    pl.semaphore_wait(barrier, len(peers))
    both(own, 0)
    both(own, 1)
    flip(2)
    flip(3)
    both(own, 2)
    flip(4)
    flip(5)
    for d in range(1, n_fib):
        early(d).start()

    for copy in whole:
        copy.wait()
    rows = lax.broadcasted_iota(jnp.int32, (8, B), 0)
    lanes = lax.broadcasted_iota(jnp.int32, (8, B), 1)
    table, place = jnp.full((8, B), S, jnp.int32), jnp.full((8, B), NO, jnp.int32)
    columns = jnp.concatenate([col_v[...], jnp.zeros((8 - R, S), jnp.int32)], axis=0)
    counts = jnp.zeros((8, B), jnp.int32)
    for r in range(R):
        counts = jnp.where(rows == r, cnt_v[r], counts)
    for s in range(S):
        offset = columns[:, s : s + 1] - (group * R + rows) + BAND
        offset = jnp.where(offset < 0, offset + n_blocks, offset)
        offset = jnp.where(offset >= n_blocks, offset - n_blocks, offset)
        table = jnp.where((offset == lanes) & (s < counts), s, table)
        place = jnp.where((lanes == s) & (s < counts), offset, place)
    tab[0:8, :] = table
    tab[8:16, :] = place

    def clear(w, _):
        Q[w, 0:BAND] = jnp.zeros((BAND, QB, B), jnp.bfloat16)
        Q[w, BAND + NO : 2 * BAND + NO] = jnp.zeros((BAND, QB, B), jnp.bfloat16)
        return 0

    lax.fori_loop(0, 3 * R, clear, 0)
    for ref in halo:
        ref[S] = jnp.zeros((QB, B), jnp.bfloat16)
    for r in range(R):
        acc[r, NO] = jnp.zeros((QB, B), jnp.float32)
        L[r][S] = jnp.zeros((B, B), jnp.bfloat16)

    local = pltpu.make_async_copy(tab, stab, loc.at[2])
    local.start()
    for r in range(R):
        both(shift, r, 0)
    tables(0).start()
    tables(1).start()
    near = (pltpu.make_async_copy(ntab.at[0], sprev, loc.at[0]), pltpu.make_async_copy(ntab.at[1], snext, loc.at[1]))

    def term(i, w):
        return Q[w, pl.ds(BAND + R + i - w, NO)].reshape(NO * QB, B), L[i][stab[i, w - i]]

    def products(i, window):
        pairs = [term(i, w) for w in window]
        right = jnp.concatenate([p[0] for p in pairs], axis=1)
        left = jnp.concatenate([p[1] for p in pairs], axis=0)
        return jnp.dot(right, left, preferred_element_type=jnp.float32).reshape(NO, QB, B)

    def within(r):
        for o in range(NO):
            Q[R + r, BAND + o] = L[r][stab[r, o], quarter]
        acc[r, 0:NO] = products(r, range(R, R + r + 1))
        for i in range(r):
            acc[i, 0:NO] += products(i, [R + r])

    def take(r):
        for o in range(NO):
            Q[r, BAND + o] = prev[r][sprev[r, o]]
            Q[2 * R + r, BAND + o] = nxt[r][snext[r, o]]

    def tell(k):
        for peer in beside:
            pl.semaphore_signal(known.at[k], inc=1, device_id=peer, device_id_type=MESH)

    tell(0)
    for r in range(R):
        drain(L[r].at[0 : 2 * T], own_r.at[r])
        both(relay, r)
        if r + 3 < R:
            both(own, r + 3)
        if r < R - 1:
            both(shift, r, 1)
            both(shift, r, n_fib - 1)
        if r == 1:
            drain(E.at[0 : S - T], e_r)
            for d in range(1, n_fib):
                both(shift, R - 1, d)
            local.wait()
        if r >= 1:
            drain(L[r].at[0:T], rel_r.at[r - 1])
            both(shift, r - 1, 2)
            within(r - 1)
        if 2 <= r < 5:
            pl.semaphore_wait(known.at[r - 2], len(beside))
            if r < 4:
                tell(r - 1)
    drain(ntab, tab_r)
    for copy in near:
        copy.start()
    drain(Q.at[0 : 2 * R, 0 : 2 * n_fib], z_r.at[0])
    for copy in near:
        copy.wait()
    for r in range(R - 2):
        take(r)
    for i in range(R - 1):
        acc[i, 0:NO] += products(i, [*range(i, R - 2), *range(2 * R, 2 * R + min(i, R - 3) + 1)])
    drain(L[R - 1].at[0:T], rel_r.at[R - 1])
    within(R - 1)
    drain(Q.at[0:R, 0 : 2 * n_fib], z_r.at[1])
    take(R - 2)
    take(R - 1)
    for i in range(R):
        late = [w for w in (R - 2, R - 1) if w >= i] + [2 * R + w for w in (R - 2, R - 1) if w <= i]
        acc[i, 0:NO] += products(i, late if i < R - 1 else [R - 1, *range(2 * R, 3 * R)])

    def deliver(i, d):
        dst = land.at[i, :, quarter]
        return remote(send.at[d - 1, i], dst, out_s, out_r.at[i], along_fib(d))

    diagonal = lax.broadcasted_iota(jnp.int32, (QB, B), 1) == lax.broadcasted_iota(jnp.int32, (QB, B), 0) + mine
    trace_values = jnp.zeros((QB, B), jnp.float32)
    trace_square = jnp.zeros((QB, B), jnp.float32)
    for i in range(R):
        trace_values += L[i][0, quarter].astype(jnp.float32)
        trace_square += acc[i, BAND]

    def total(tile):
        return jnp.sum(jnp.where(diagonal, tile, 0.0), axis=0, keepdims=True)

    place_x = 2 * fib + core
    tx[place_x] = jnp.where(rows == 0, total(trace_values), jnp.where(rows == 1, total(trace_square), 0.0))

    def spread(buf, me, size, ssem, rsem, device):
        return [remote(buf.at[me], buf.at[me], ssem, rsem, device(d)) for d in range(1, size)]

    def add(buf, size):
        tile = buf[0]
        for k in range(1, size):
            tile += buf[k]
        return tile

    stage_x = spread(tx, place_x, 2 * n_fib, tx_s, tx_r, along_line)
    stage_z = spread(tz, col, n_col, tz_s, tz_r, along_col)
    stage_y = spread(ty, row // 2, n_row // 2, ty_s, ty_r, lambda d: along_row(2 * d))
    for i in range(R):
        for d in range(n_fib):
            owner = lax.rem(fib + d, n_fib)
            for t in range(T):
                block = acc[i, stab[8 + i, T * owner + t]].astype(jnp.bfloat16)
                if d == 0:
                    land[i, t, quarter] = block
                else:
                    send[d - 1, i, t] = block
        if i == 0:
            for copy in stage_x:
                copy.start()
        else:
            for d in range(1, n_fib):
                deliver(i - 1, d).start()
        if i == R // 2:
            drain(tx.at[1 : 2 * n_fib], tx_r)
            tz[col] = add(tx, 2 * n_fib)
            for copy in stage_z:
                copy.start()
    for d in range(1, n_fib):
        deliver(R - 1, d).start()
    drain(tz.at[1:n_col], tz_r)
    ty[row // 2] = add(tz, n_col)
    for copy in stage_y:
        copy.start()

    drain(Q.at[:, 0 : 2 * n_fib], own_s)
    drain(Q.at[:, 0:n_fib], rel_s)
    drain(Q.at[:, 0 : 2 * n_fib], z_s)
    drain(E.at[0 : S - T], e_s)
    drain(tab, tab_s)
    drain(send, out_s)
    drain(tx.at[1 : 2 * n_fib], tx_s)
    drain(tz.at[1:n_col], tz_s)
    for i in range(R):
        drain(land.at[i, :, 0 : B - QB], out_r.at[i])
    drain(ty.at[1 : n_row // 2], ty_r)
    drain(ty.at[1 : n_row // 2], ty_s)


def finish(land, ty, out_ref, tr_ref, out_v, sem):
    copies = []
    for i in range(R):
        for t in range(T):
            out_v[i, t] = land[i, t].T
        copies.append(pltpu.make_async_copy(out_v.at[i], out_ref.at[i], sem.at[i]))
        if i:
            copies[i - 1].start()
    copies[R - 1].start()
    sums = ty[0]
    for k in range(1, ty.shape[0]):
        sums += ty[k]
    tr_ref[0] = jnp.sum(sums[0:1])
    tr_ref[1] = jnp.sum(sums[1:2])
    for copy in copies:
        copy.wait()


def solution(mesh):
    sizes = tuple(mesh.shape[a] for a in ("row", "col", "fib"))
    bf16, f32, i32 = jnp.bfloat16, jnp.float32, jnp.int32
    dma = pltpu.SemaphoreType.DMA

    def body(values, columns, counts):
        vmem, smem = pl.BlockSpec(memory_space=pltpu.VMEM), pl.BlockSpec(memory_space=pltpu.SMEM)
        hbm = pl.BlockSpec(memory_space=pl.ANY)
        land, ty = pl.pallas_call(
            functools.partial(kernel, sizes),
            out_shape=(pltpu.VMEM((R, T, B, B), bf16), pltpu.VMEM((sizes[0] // 2, 8, B), f32)),
            in_specs=[hbm, hbm, hbm],
            out_specs=(vmem, vmem),
            scratch_shapes=[
                pltpu.VMEM((R, T, B, B), bf16),
                pltpu.VMEM((R, S), i32),
                pltpu.SMEM((R,), i32),
                pltpu.VMEM((S, QB, B), bf16),
                pltpu.VMEM((3 * R, NO + 2 * BAND, QB, B), bf16),
                pltpu.VMEM((R, NO + 1, QB, B), f32),
                pltpu.VMEM((3, R, T, QB, B), bf16),
                pltpu.VMEM((16, B), i32),
                pltpu.VMEM((2, 8, B), i32),
                pltpu.VMEM((2 * sizes[2], 8, B), f32),
                pltpu.VMEM((sizes[1], 8, B), f32),
                pltpu.SMEM((16, B), i32),
                pltpu.SMEM((8, B), i32),
                pltpu.SMEM((8, B), i32),
                dma((R,)),
                dma((3,)),
                dma((R,)),
                dma((R,)),
                dma((2,)),
                dma((R,)),
                dma((14,)),
                pltpu.SemaphoreType.REGULAR((3,)),
                *[pltpu.VMEM((S + 1, B, B), bf16)] * R,
                *[pltpu.VMEM((S + 1, QB, B), bf16)] * (2 * R),
            ],
            compiler_params=pltpu.CompilerParams(collective_id=0, has_side_effects=True),
        )(values, columns, counts)
        return pl.pallas_call(
            finish,
            out_shape=(jax.ShapeDtypeStruct((R, T, B, B), bf16), jax.ShapeDtypeStruct((2,), f32)),
            in_specs=[vmem, vmem],
            out_specs=(hbm, smem),
            scratch_shapes=[pltpu.VMEM((R, T, B, B), bf16), dma((R,))],
        )(*(pltpu.with_memory_space_constraint(a, pltpu.VMEM) for a in (land, ty)))

    in_specs = (P(("row", "col"), "fib", None, None), P(("row", "col"), None), P(("row", "col")))
    out_specs = (P(("row", "col"), "fib", None, None), P())
    return jax.shard_map(body, mesh=mesh, in_specs=in_specs, out_specs=out_specs, check_vma=False)
```

```python
import functools

import jax
import jax.numpy as jnp
from jax import lax
from jax.experimental import pallas as pl
from jax.experimental.pallas import tpu as pltpu
from jax.sharding import PartitionSpec as P

MESH = pl.DeviceIdType.MESH
BAND = 6
R = 6
T = 3
S = 12
NO = 2 * BAND + 1
B = 128
QB = 32


def kernel(sizes, v_ref, col_ref, cnt_ref, turned, ty, held, land, col_v, cnt_v, E, Q, acc, send, tab, ntab, tx, tz,
           stab, sprev, snext, held_s, loc, own_r, rel_r, z_r, out_r, once, known, *buffers):
    n_row, n_col, n_fib = sizes
    n_blocks = n_row * n_col * R
    row, col, fib = (lax.axis_index(a) for a in ("row", "col", "fib"))
    group = row * n_col + col

    def along_fib(d):
        return (row, col, lax.rem(fib + d + n_fib, n_fib))

    def along_col(d):
        return (row, lax.rem(col + d, n_col), fib)

    def along_row(d):
        return (lax.rem(row + d, n_row), col, fib)

    def along_group(d):
        other = lax.rem(group + d + n_row * n_col, n_row * n_col)
        return (other // n_col, lax.rem(other, n_col), fib)

    beside = [along_col(1), along_col(n_col - 1), *(along_row(d) for d in (1, 2, n_row - 2, n_row - 1))]
    core = lax.rem(row, 2)

    def along_line(d):
        return (row - core + lax.rem(core + d, 2), col, lax.rem(fib + d // 2, n_fib))

    peers = [along_line(d) for d in range(1, 2 * n_fib)] + [along_fib(d) for d in range(1, n_fib)] + [along_group(1), along_group(-1)] + beside
    fetches = [pltpu.make_async_copy(v_ref.at[r], held.at[r], held_s.at[r]) for r in range(R)]
    fetches[0].start()
    fetches[1].start()
    barrier = pltpu.get_barrier_semaphore()
    for peer in peers:
        pl.semaphore_signal(barrier, inc=1, device_id=peer, device_id_type=MESH)

    def remote(src, dst, ssem, rsem, device):
        return pltpu.make_async_remote_copy(
            src_ref=src, dst_ref=dst, send_sem=ssem, recv_sem=rsem, device_id=device, device_id_type=MESH
        )

    mine = pl.multiple_of(fib * QB, QB)
    quarter = pl.ds(mine, QB)
    L, halo = buffers[:R], buffers[R:]
    prev, nxt = halo[:R], halo[R:]

    (own_s, rel_s, z_s, tab_s, tab_r, out_s, tx_s, tx_r, tz_s, tz_r, ty_s, ty_r, e_s, e_r) = (
        once.at[k] for k in range(14)
    )
    whole = [
        pltpu.make_async_copy(col_ref, col_v, loc.at[0]),
        pltpu.make_async_copy(cnt_ref, cnt_v, loc.at[1]),
    ]
    for fetch in fetches[2:] + whole:
        fetch.start()

    def flip(r):
        fetches[r].wait()
        for t in range(T):
            L[r][T * fib + t] = held[r, t].T

    def own(r, way):
        part = L[r].at[pl.ds(T * fib, T)]
        return remote(part, part, own_s, own_r.at[r], along_fib(1 - 2 * way))

    def relay(r, way):
        cut = 2 - r % 2
        source = lax.rem(fib + (n_fib - 1 if way == 0 else 1), n_fib)
        part = L[r].at[pl.ds(T * source, cut)] if way == 0 else L[r].at[pl.ds(T * source + cut, T - cut)]
        return remote(part, part, rel_s, rel_r.at[r], along_fib(1 - 2 * way))

    def shift(r, way, d):
        part = pl.ds(T * lax.rem(fib + d, n_fib), T)
        dst = (prev if way == 0 else nxt)[r].at[part]
        src = E.at[part] if r == R - 1 and d == 2 else L[r].at[part, quarter]
        return remote(src, dst, z_s, z_r.at[r // (R - 2)], along_group(1 - 2 * way))

    def early(d):
        theirs = pl.ds(pl.multiple_of(lax.rem(fib + d, n_fib) * QB, QB), QB)
        part = pl.ds(T * fib, T)
        return remote(L[R - 1].at[part, theirs], E.at[part], e_s, e_r, along_fib(d))

    def drain(ref, sem):
        pltpu.make_async_copy(ref, ref, sem).wait()

    def both(make, *where):
        make(*where[:1], 0, *where[1:]).start()
        make(*where[:1], 1, *where[1:]).start()

    def tables(way):
        return remote(tab.at[0:8], ntab.at[way], tab_s, tab_r, along_group(1 - 2 * way))

    flip(0)
    flip(1)
    pl.semaphore_wait(barrier, len(peers))
    both(own, 0)
    both(own, 1)
    flip(2)
    flip(3)
    both(own, 2)
    flip(4)
    flip(5)
    early(2).start()

    for copy in whole:
        copy.wait()
    rows = lax.broadcasted_iota(jnp.int32, (8, B), 0)
    lanes = lax.broadcasted_iota(jnp.int32, (8, B), 1)
    table, place = jnp.full((8, B), S, jnp.int32), jnp.full((8, B), NO, jnp.int32)
    columns = jnp.concatenate([col_v[...], jnp.zeros((8 - R, S), jnp.int32)], axis=0)
    counts = jnp.zeros((8, B), jnp.int32)
    for r in range(R):
        counts = jnp.where(rows == r, cnt_v[r], counts)
    for s in range(S):
        offset = columns[:, s : s + 1] - (group * R + rows) + BAND
        offset = jnp.where(offset < 0, offset + n_blocks, offset)
        offset = jnp.where(offset >= n_blocks, offset - n_blocks, offset)
        table = jnp.where((offset == lanes) & (s < counts), s, table)
        place = jnp.where((lanes == s) & (s < counts), offset, place)
    tab[0:8, :] = table
    tab[8:16, :] = place

    def clear(w, _):
        Q[w, 0:BAND] = jnp.zeros((BAND, QB, B), jnp.bfloat16)
        Q[w, BAND + NO : 2 * BAND + NO] = jnp.zeros((BAND, QB, B), jnp.bfloat16)
        return 0

    lax.fori_loop(0, 3 * R, clear, 0)
    for ref in halo:
        ref[S] = jnp.zeros((QB, B), jnp.bfloat16)
    for r in range(R):
        acc[r, NO] = jnp.zeros((QB, B), jnp.float32)
        L[r][S] = jnp.zeros((B, B), jnp.bfloat16)

    local = pltpu.make_async_copy(tab, stab, loc.at[2])
    local.start()
    for r in range(R):
        both(shift, r, 0)
    tables(0).start()
    tables(1).start()
    near = (pltpu.make_async_copy(ntab.at[0], sprev, loc.at[0]), pltpu.make_async_copy(ntab.at[1], snext, loc.at[1]))

    def term(i, w):
        return Q[w, pl.ds(BAND + R + i - w, NO)].reshape(NO * QB, B), L[i][stab[i, w - i]]

    def products(i, window):
        pairs = [term(i, w) for w in window]
        right = jnp.concatenate([p[0] for p in pairs], axis=1)
        left = jnp.concatenate([p[1] for p in pairs], axis=0)
        return jnp.dot(right, left, preferred_element_type=jnp.float32).reshape(NO, QB, B)

    def within(r):
        for o in range(NO):
            Q[R + r, BAND + o] = L[r][stab[r, o], quarter]
        acc[r, 0:NO] = products(r, range(R, R + r + 1))
        for i in range(r):
            acc[i, 0:NO] += products(i, [R + r])

    def take(r):
        for o in range(NO):
            Q[r, BAND + o] = prev[r][sprev[r, o]]
            Q[2 * R + r, BAND + o] = nxt[r][snext[r, o]]

    def tell(k):
        for peer in beside:
            pl.semaphore_signal(known.at[k], inc=1, device_id=peer, device_id_type=MESH)

    tell(0)
    for r in range(R):
        drain(L[r].at[0 : 2 * T], own_r.at[r])
        both(relay, r)
        if r + 3 < R:
            both(own, r + 3)
        both(shift, r, 1)
        both(shift, r, n_fib - 1)
        if r == 1:
            drain(E.at[0:T], e_r)
            both(shift, R - 1, 2)
            local.wait()
        if r >= 1:
            drain(L[r].at[0:T], rel_r.at[r - 1])
            both(shift, r - 1, 2)
            within(r - 1)
        if 2 <= r < 5:
            pl.semaphore_wait(known.at[r - 2], len(beside))
            if r < 4:
                tell(r - 1)
    drain(ntab, tab_r)
    for copy in near:
        copy.start()
    drain(Q.at[0 : 2 * R, 0 : 2 * n_fib], z_r.at[0])
    for copy in near:
        copy.wait()
    for r in range(R - 2):
        take(r)
    for i in range(R - 1):
        acc[i, 0:NO] += products(i, [*range(i, R - 2), *range(2 * R, 2 * R + min(i, R - 3) + 1)])
    drain(L[R - 1].at[0:T], rel_r.at[R - 1])
    within(R - 1)
    drain(Q.at[0:R, 0 : 2 * n_fib], z_r.at[1])
    take(R - 2)
    take(R - 1)
    for i in range(R):
        late = [w for w in (R - 2, R - 1) if w >= i] + [2 * R + w for w in (R - 2, R - 1) if w <= i]
        acc[i, 0:NO] += products(i, late if i < R - 1 else [R - 1, *range(2 * R, 3 * R)])

    def deliver(i, d):
        dst = land.at[i, :, quarter]
        return remote(send.at[d - 1, i], dst, out_s, out_r.at[i], along_fib(d))

    diagonal = lax.broadcasted_iota(jnp.int32, (QB, B), 1) == lax.broadcasted_iota(jnp.int32, (QB, B), 0) + mine
    trace_values = jnp.zeros((QB, B), jnp.float32)
    trace_square = jnp.zeros((QB, B), jnp.float32)
    for i in range(R):
        trace_values += L[i][0, quarter].astype(jnp.float32)
        trace_square += acc[i, BAND]

    def total(tile):
        return jnp.sum(jnp.where(diagonal, tile, 0.0), axis=0, keepdims=True)

    place_x = 2 * fib + core
    tx[place_x] = jnp.where(rows == 0, total(trace_values), jnp.where(rows == 1, total(trace_square), 0.0))

    def spread(buf, me, size, ssem, rsem, device):
        return [remote(buf.at[me], buf.at[me], ssem, rsem, device(d)) for d in range(1, size)]

    def add(buf, size):
        tile = buf[0]
        for k in range(1, size):
            tile += buf[k]
        return tile

    stage_x = spread(tx, place_x, 2 * n_fib, tx_s, tx_r, along_line)
    stage_z = spread(tz, col, n_col, tz_s, tz_r, along_col)
    stage_y = spread(ty, row // 2, n_row // 2, ty_s, ty_r, lambda d: along_row(2 * d))
    for i in range(R):
        for d in range(n_fib):
            owner = lax.rem(fib + d, n_fib)
            for t in range(T):
                block = acc[i, stab[8 + i, T * owner + t]].astype(jnp.bfloat16)
                if d == 0:
                    land[i, t, quarter] = block
                else:
                    send[d - 1, i, t] = block
        if i == 0:
            for copy in stage_x:
                copy.start()
        else:
            for d in range(1, n_fib):
                deliver(i - 1, d).start()
        if i == R // 2:
            drain(tx.at[1 : 2 * n_fib], tx_r)
            tz[col] = add(tx, 2 * n_fib)
            for copy in stage_z:
                copy.start()
    for d in range(1, n_fib):
        deliver(R - 1, d).start()
    drain(tz.at[1:n_col], tz_r)
    ty[row // 2] = add(tz, n_col)
    for copy in stage_y:
        copy.start()

    drain(Q.at[:, 0 : 2 * n_fib], own_s)
    drain(Q.at[:, 0:n_fib], rel_s)
    drain(Q.at[:, 0 : 2 * n_fib], z_s)
    drain(E.at[0:T], e_s)
    drain(tab, tab_s)
    drain(send, out_s)
    drain(tx.at[1 : 2 * n_fib], tx_s)
    drain(tz.at[1:n_col], tz_s)
    for i in range(R):
        drain(land.at[i, :, 0 : B - QB], out_r.at[i])
        for t in range(T):
            turned[i, t] = land[i, t].T
    drain(ty.at[1 : n_row // 2], ty_r)
    drain(ty.at[1 : n_row // 2], ty_s)


def finish(turned, ty, out_ref, tr_ref, sem):
    copies = [pltpu.make_async_copy(turned.at[i], out_ref.at[i], sem.at[i]) for i in range(R)]
    for copy in copies:
        copy.start()
    sums = ty[0]
    for k in range(1, ty.shape[0]):
        sums += ty[k]
    tr_ref[0] = jnp.sum(sums[0:1])
    tr_ref[1] = jnp.sum(sums[1:2])
    for copy in copies:
        copy.wait()


def solution(mesh):
    sizes = tuple(mesh.shape[a] for a in ("row", "col", "fib"))
    bf16, f32, i32 = jnp.bfloat16, jnp.float32, jnp.int32
    dma = pltpu.SemaphoreType.DMA

    def body(values, columns, counts):
        vmem, smem = pl.BlockSpec(memory_space=pltpu.VMEM), pl.BlockSpec(memory_space=pltpu.SMEM)
        hbm = pl.BlockSpec(memory_space=pl.ANY)
        turned, ty = pl.pallas_call(
            functools.partial(kernel, sizes),
            out_shape=(pltpu.VMEM((R, T, B, B), bf16), pltpu.VMEM((sizes[0] // 2, 8, B), f32)),
            in_specs=[hbm, hbm, hbm],
            out_specs=(vmem, vmem),
            scratch_shapes=[
                pltpu.VMEM((R, T, B, B), bf16),
                pltpu.VMEM((R, T, B, B), bf16),
                pltpu.VMEM((R, S), i32),
                pltpu.SMEM((R,), i32),
                pltpu.VMEM((S, QB, B), bf16),
                pltpu.VMEM((3 * R, NO + 2 * BAND, QB, B), bf16),
                pltpu.VMEM((R, NO + 1, QB, B), f32),
                pltpu.VMEM((3, R, T, QB, B), bf16),
                pltpu.VMEM((16, B), i32),
                pltpu.VMEM((2, 8, B), i32),
                pltpu.VMEM((2 * sizes[2], 8, B), f32),
                pltpu.VMEM((sizes[1], 8, B), f32),
                pltpu.SMEM((16, B), i32),
                pltpu.SMEM((8, B), i32),
                pltpu.SMEM((8, B), i32),
                dma((R,)),
                dma((3,)),
                dma((R,)),
                dma((R,)),
                dma((2,)),
                dma((R,)),
                dma((14,)),
                pltpu.SemaphoreType.REGULAR((3,)),
                *[pltpu.VMEM((S + 1, B, B), bf16)] * R,
                *[pltpu.VMEM((S + 1, QB, B), bf16)] * (2 * R),
            ],
            compiler_params=pltpu.CompilerParams(collective_id=0, has_side_effects=True),
        )(values, columns, counts)
        return pl.pallas_call(
            finish,
            out_shape=(jax.ShapeDtypeStruct((R, T, B, B), bf16), jax.ShapeDtypeStruct((2,), f32)),
            in_specs=[vmem, vmem],
            out_specs=(hbm, smem),
            scratch_shapes=[dma((R,))],
        )(*(pltpu.with_memory_space_constraint(a, pltpu.VMEM) for a in (turned, ty)))

    in_specs = (P(("row", "col"), "fib", None, None), P(("row", "col"), None), P(("row", "col")))
    out_specs = (P(("row", "col"), "fib", None, None), P())
    return jax.shard_map(body, mesh=mesh, in_specs=in_specs, out_specs=out_specs, check_vma=False)
```

```python
import functools

import jax
import jax.numpy as jnp
from jax import lax
from jax.experimental import pallas as pl
from jax.experimental.pallas import tpu as pltpu
from jax.sharding import PartitionSpec as P

MESH = pl.DeviceIdType.MESH
BAND = 6
R = 6
T = 3
S = 12
NO = 2 * BAND + 1
B = 128
QB = 32


def kernel(sizes, v_ref, col_ref, cnt_ref, turned, ty, held, land, col_v, cnt_v, E, Q, acc, send, tab, ntab, tx, tz,
           stab, sprev, snext, held_s, loc, own_r, rel_r, z_r, out_r, once, known, *buffers):
    n_row, n_col, n_fib = sizes
    n_blocks = n_row * n_col * R
    row, col, fib = (lax.axis_index(a) for a in ("row", "col", "fib"))
    group = row * n_col + col

    def along_fib(d):
        return (row, col, lax.rem(fib + d + n_fib, n_fib))

    def along_col(d):
        return (row, lax.rem(col + d, n_col), fib)

    def along_row(d):
        return (lax.rem(row + d, n_row), col, fib)

    def along_group(d):
        other = lax.rem(group + d + n_row * n_col, n_row * n_col)
        return (other // n_col, lax.rem(other, n_col), fib)

    beside = [along_col(1), along_col(n_col - 1), *(along_row(d) for d in (1, 2, n_row - 2, n_row - 1))]
    core = lax.rem(row, 2)

    def along_line(d):
        return (row - core + lax.rem(core + d, 2), col, lax.rem(fib + d // 2, n_fib))

    peers = [along_line(d) for d in range(1, 2 * n_fib)] + [along_group(1), along_group(-1)] + beside
    fetches = [pltpu.make_async_copy(v_ref.at[r], held.at[r], held_s.at[r]) for r in range(R)]
    fetches[0].start()
    fetches[1].start()
    barrier = pltpu.get_barrier_semaphore()
    for peer in peers:
        pl.semaphore_signal(barrier, inc=1, device_id=peer, device_id_type=MESH)

    def remote(src, dst, ssem, rsem, device):
        return pltpu.make_async_remote_copy(
            src_ref=src, dst_ref=dst, send_sem=ssem, recv_sem=rsem, device_id=device, device_id_type=MESH
        )

    mine = pl.multiple_of(fib * QB, QB)
    quarter = pl.ds(mine, QB)
    L, halo = buffers[:R], buffers[R:]
    prev, nxt = halo[:R], halo[R:]

    (own_s, rel_s, z_s, tab_s, tab_r, out_s, tx_s, tx_r, tz_s, tz_r, ty_s, ty_r, e_s, e_r) = (
        once.at[k] for k in range(14)
    )
    whole = [
        pltpu.make_async_copy(col_ref, col_v, loc.at[0]),
        pltpu.make_async_copy(cnt_ref, cnt_v, loc.at[1]),
    ]
    for fetch in fetches[2:] + whole:
        fetch.start()

    def flip(r):
        fetches[r].wait()
        for t in range(T):
            L[r][T * fib + t] = held[r, t].T

    def own(r, way):
        part = L[r].at[pl.ds(T * fib, T)]
        return remote(part, part, own_s, own_r.at[r], along_fib(1 - 2 * way))

    def relay(r, way):
        cut = 2 - r % 2
        source = lax.rem(fib + (n_fib - 1 if way == 0 else 1), n_fib)
        part = L[r].at[pl.ds(T * source, cut)] if way == 0 else L[r].at[pl.ds(T * source + cut, T - cut)]
        return remote(part, part, rel_s, rel_r.at[r], along_fib(1 - 2 * way))

    def shift(r, way, d):
        part = pl.ds(T * lax.rem(fib + d, n_fib), T)
        dst = (prev if way == 0 else nxt)[r].at[part]
        src = E.at[part] if r == R - 1 and d == 2 else L[r].at[part, quarter]
        return remote(src, dst, z_s, z_r.at[r // (R - 2)], along_group(1 - 2 * way))

    def early(d):
        theirs = pl.ds(pl.multiple_of(lax.rem(fib + d, n_fib) * QB, QB), QB)
        part = pl.ds(T * fib, T)
        return remote(L[R - 1].at[part, theirs], E.at[part], e_s, e_r, along_fib(d))

    def drain(ref, sem):
        pltpu.make_async_copy(ref, ref, sem).wait()

    def both(make, *where):
        make(*where[:1], 0, *where[1:]).start()
        make(*where[:1], 1, *where[1:]).start()

    def tables(way):
        return remote(tab.at[0:8], ntab.at[way], tab_s, tab_r, along_group(1 - 2 * way))

    flip(0)
    flip(1)
    pl.semaphore_wait(barrier, len(peers))
    both(own, 0)
    both(own, 1)
    flip(2)
    flip(3)
    both(own, 2)
    flip(4)
    flip(5)
    early(2).start()

    for copy in whole:
        copy.wait()
    rows = lax.broadcasted_iota(jnp.int32, (8, B), 0)
    lanes = lax.broadcasted_iota(jnp.int32, (8, B), 1)
    table, place = jnp.full((8, B), S, jnp.int32), jnp.full((8, B), NO, jnp.int32)
    columns = jnp.concatenate([col_v[...], jnp.zeros((8 - R, S), jnp.int32)], axis=0)
    counts = jnp.zeros((8, B), jnp.int32)
    for r in range(R):
        counts = jnp.where(rows == r, cnt_v[r], counts)
    for s in range(S):
        offset = columns[:, s : s + 1] - (group * R + rows) + BAND
        offset = jnp.where(offset < 0, offset + n_blocks, offset)
        offset = jnp.where(offset >= n_blocks, offset - n_blocks, offset)
        table = jnp.where((offset == lanes) & (s < counts), s, table)
        place = jnp.where((lanes == s) & (s < counts), offset, place)
    tab[0:8, :] = table
    tab[8:16, :] = place

    def clear(w, _):
        Q[w, 0:BAND] = jnp.zeros((BAND, QB, B), jnp.bfloat16)
        Q[w, BAND + NO : 2 * BAND + NO] = jnp.zeros((BAND, QB, B), jnp.bfloat16)
        return 0

    lax.fori_loop(0, 3 * R, clear, 0)
    for ref in halo:
        ref[S] = jnp.zeros((QB, B), jnp.bfloat16)
    for r in range(R):
        acc[r, NO] = jnp.zeros((QB, B), jnp.float32)
        L[r][S] = jnp.zeros((B, B), jnp.bfloat16)

    local = pltpu.make_async_copy(tab, stab, loc.at[2])
    local.start()
    for r in range(R):
        both(shift, r, 0)
    tables(0).start()
    tables(1).start()
    near = (pltpu.make_async_copy(ntab.at[0], sprev, loc.at[0]), pltpu.make_async_copy(ntab.at[1], snext, loc.at[1]))

    def term(i, w):
        return Q[w, pl.ds(BAND + R + i - w, NO)].reshape(NO * QB, B), L[i][stab[i, w - i]]

    def products(i, window):
        pairs = [term(i, w) for w in window]
        right = jnp.concatenate([p[0] for p in pairs], axis=1)
        left = jnp.concatenate([p[1] for p in pairs], axis=0)
        return jnp.dot(right, left, preferred_element_type=jnp.float32).reshape(NO, QB, B)

    def within(r):
        for o in range(NO):
            Q[R + r, BAND + o] = L[r][stab[r, o], quarter]
        acc[r, 0:NO] = products(r, range(R, R + r + 1))
        for i in range(r):
            acc[i, 0:NO] += products(i, [R + r])

    def take(r):
        for o in range(NO):
            Q[r, BAND + o] = prev[r][sprev[r, o]]
            Q[2 * R + r, BAND + o] = nxt[r][snext[r, o]]

    def tell(k):
        for peer in beside:
            pl.semaphore_signal(known.at[k], inc=1, device_id=peer, device_id_type=MESH)

    tell(0)
    for r in range(R):
        drain(L[r].at[0 : 2 * T], own_r.at[r])
        both(relay, r)
        if r + 3 < R:
            both(own, r + 3)
        both(shift, r, 1)
        both(shift, r, n_fib - 1)
        if r == R - 1:
            drain(ntab, tab_r)
            for copy in near:
                copy.start()
        if r == 1:
            drain(E.at[0:T], e_r)
            both(shift, R - 1, 2)
            local.wait()
        if r >= 1:
            drain(L[r].at[0:T], rel_r.at[r - 1])
            both(shift, r - 1, 2)
            within(r - 1)
        if 2 <= r < 5:
            pl.semaphore_wait(known.at[r - 2], len(beside))
            if r < 4:
                tell(r - 1)
    drain(Q.at[0 : 2 * R, 0 : 2 * n_fib], z_r.at[0])
    for copy in near:
        copy.wait()
    for r in range(R - 2):
        take(r)
    for i in range(R - 1):
        acc[i, 0:NO] += products(i, [*range(i, R - 2), *range(2 * R, 2 * R + min(i, R - 3) + 1)])
    drain(L[R - 1].at[0:T], rel_r.at[R - 1])
    within(R - 1)
    drain(Q.at[0:R, 0 : 2 * n_fib], z_r.at[1])
    take(R - 2)
    take(R - 1)
    for i in range(R):
        late = [w for w in (R - 2, R - 1) if w >= i] + [2 * R + w for w in (R - 2, R - 1) if w <= i]
        acc[i, 0:NO] += products(i, late if i < R - 1 else [R - 1, *range(2 * R, 3 * R)])

    def deliver(i, d):
        dst = land.at[i, :, quarter]
        return remote(send.at[d - 1, i], dst, out_s, out_r.at[i], along_fib(d))

    diagonal = lax.broadcasted_iota(jnp.int32, (QB, B), 1) == lax.broadcasted_iota(jnp.int32, (QB, B), 0) + mine
    trace_values = jnp.zeros((QB, B), jnp.float32)
    trace_square = jnp.zeros((QB, B), jnp.float32)
    for i in range(R):
        trace_values += L[i][0, quarter].astype(jnp.float32)
        trace_square += acc[i, BAND]

    def total(tile):
        return jnp.sum(jnp.where(diagonal, tile, 0.0), axis=0, keepdims=True)

    place_x = 2 * fib + core
    tx[place_x] = jnp.where(rows == 0, total(trace_values), jnp.where(rows == 1, total(trace_square), 0.0))

    def spread(buf, me, size, ssem, rsem, device):
        return [remote(buf.at[me], buf.at[me], ssem, rsem, device(d)) for d in range(1, size)]

    def add(buf, size):
        tile = buf[0]
        for k in range(1, size):
            tile += buf[k]
        return tile

    stage_x = spread(tx, place_x, 2 * n_fib, tx_s, tx_r, along_line)
    stage_z = spread(tz, col, n_col, tz_s, tz_r, along_col)
    stage_y = spread(ty, row // 2, n_row // 2, ty_s, ty_r, lambda d: along_row(2 * d))
    for i in range(R):
        for d in range(n_fib):
            owner = lax.rem(fib + d, n_fib)
            for t in range(T):
                block = acc[i, stab[8 + i, T * owner + t]].astype(jnp.bfloat16)
                if d == 0:
                    land[i, t, quarter] = block
                else:
                    send[d - 1, i, t] = block
        if i == 0:
            for copy in stage_x:
                copy.start()
        else:
            for d in range(1, n_fib):
                deliver(i - 1, d).start()
        if i == R // 2:
            drain(tx.at[1 : 2 * n_fib], tx_r)
            tz[col] = add(tx, 2 * n_fib)
            for copy in stage_z:
                copy.start()
    for d in range(1, n_fib):
        deliver(R - 1, d).start()
    drain(tz.at[1:n_col], tz_r)
    ty[row // 2] = add(tz, n_col)
    for copy in stage_y:
        copy.start()

    drain(Q.at[:, 0 : 2 * n_fib], own_s)
    drain(Q.at[:, 0:n_fib], rel_s)
    drain(Q.at[:, 0 : 2 * n_fib], z_s)
    drain(E.at[0:T], e_s)
    drain(tab, tab_s)
    drain(send, out_s)
    drain(tx.at[1 : 2 * n_fib], tx_s)
    drain(tz.at[1:n_col], tz_s)
    for i in range(R):
        drain(land.at[i, :, 0 : B - QB], out_r.at[i])
        for t in range(T):
            turned[i, t] = land[i, t].T
    drain(ty.at[1 : n_row // 2], ty_r)
    drain(ty.at[1 : n_row // 2], ty_s)


def finish(turned, ty, out_ref, tr_ref, sem):
    copies = [pltpu.make_async_copy(turned.at[i], out_ref.at[i], sem.at[i]) for i in range(R)]
    for copy in copies:
        copy.start()
    sums = ty[0]
    for k in range(1, ty.shape[0]):
        sums += ty[k]
    tr_ref[0] = jnp.sum(sums[0:1])
    tr_ref[1] = jnp.sum(sums[1:2])
    for copy in copies:
        copy.wait()


def solution(mesh):
    sizes = tuple(mesh.shape[a] for a in ("row", "col", "fib"))
    bf16, f32, i32 = jnp.bfloat16, jnp.float32, jnp.int32
    dma = pltpu.SemaphoreType.DMA

    def body(values, columns, counts):
        vmem, smem = pl.BlockSpec(memory_space=pltpu.VMEM), pl.BlockSpec(memory_space=pltpu.SMEM)
        hbm = pl.BlockSpec(memory_space=pl.ANY)
        turned, ty = pl.pallas_call(
            functools.partial(kernel, sizes),
            out_shape=(pltpu.VMEM((R, T, B, B), bf16), pltpu.VMEM((sizes[0] // 2, 8, B), f32)),
            in_specs=[hbm, hbm, hbm],
            out_specs=(vmem, vmem),
            scratch_shapes=[
                pltpu.VMEM((R, T, B, B), bf16),
                pltpu.VMEM((R, T, B, B), bf16),
                pltpu.VMEM((R, S), i32),
                pltpu.SMEM((R,), i32),
                pltpu.VMEM((S, QB, B), bf16),
                pltpu.VMEM((3 * R, NO + 2 * BAND, QB, B), bf16),
                pltpu.VMEM((R, NO + 1, QB, B), f32),
                pltpu.VMEM((3, R, T, QB, B), bf16),
                pltpu.VMEM((16, B), i32),
                pltpu.VMEM((2, 8, B), i32),
                pltpu.VMEM((2 * sizes[2], 8, B), f32),
                pltpu.VMEM((sizes[1], 8, B), f32),
                pltpu.SMEM((16, B), i32),
                pltpu.SMEM((8, B), i32),
                pltpu.SMEM((8, B), i32),
                dma((R,)),
                dma((3,)),
                dma((R,)),
                dma((R,)),
                dma((2,)),
                dma((R,)),
                dma((14,)),
                pltpu.SemaphoreType.REGULAR((3,)),
                *[pltpu.VMEM((S + 1, B, B), bf16)] * R,
                *[pltpu.VMEM((S + 1, QB, B), bf16)] * (2 * R),
            ],
            compiler_params=pltpu.CompilerParams(collective_id=0, has_side_effects=True),
        )(values, columns, counts)
        return pl.pallas_call(
            finish,
            out_shape=(jax.ShapeDtypeStruct((R, T, B, B), bf16), jax.ShapeDtypeStruct((2,), f32)),
            in_specs=[vmem, vmem],
            out_specs=(hbm, smem),
            scratch_shapes=[dma((R,))],
        )(*(pltpu.with_memory_space_constraint(a, pltpu.VMEM) for a in (turned, ty)))

    in_specs = (P(("row", "col"), "fib", None, None), P(("row", "col"), None), P(("row", "col")))
    out_specs = (P(("row", "col"), "fib", None, None), P())
    return jax.shard_map(body, mesh=mesh, in_specs=in_specs, out_specs=out_specs, check_vma=False)
```
